512 devices in a mesh: pool: 64 (over y, z), tensor: 8 (over x, core).
Axes of the slice: x: 4, y: 8, z: 8, core: 2. Of those that a mesh axis runs over, the one named last changes fastest.
Arguments:
- tokens: bfloat16 [2, 256, 8192], P(None, None, 'tensor'), may hold values from -6 to 6
- gate_up_weight: bfloat16 [8192, 2, 28672], P('tensor', None, 'pool'), may hold values from -0.0625 to 0.0625
- down_weight: bfloat16 [28672, 8192], P('pool', 'tensor'), may hold values from -0.03125 to 0.03125
- shrink_store: bfloat16 [64, 2, 8192, 64], P('pool', None, 'tensor'), may hold values from -0.0625 to 0.0625
- expand_store: bfloat16 [64, 2, 64, 28672], P('pool', None, 'tensor'), may hold values from -0.75 to 0.75
- block_adapter: int32 [2, 2], replicated, may hold values from 0 to 63
- block_live: int32 [2, 2], replicated, may hold values from 1 to 128, 192 in all within a row
- adapter_slot: int32 [64], replicated, may hold values from 0 to 63, each once
Outputs:
- layer_out: bfloat16 [2, 256, 8192], P(None, 'pool', 'tensor')
The draws below stay inside these ranges and needn't reach their ends.
Inputs may be any that keep to these rules, and one draw needn't show every extreme that they name: Each storage slot holds exactly one adapter; adapter a is stored on index adapter_slot[a] of pool; each index of pool holds exactly one storage slot. `block_live`: rows of a block after its live rows are padding; the live rows of one decode step sum to 192.
All inputs are finite; a program needn't handle non-finite values.
Results may differ from the reference program's by a relative error of at most 0.0049.
Values may be sent and summed in bfloat16 or wider, within the bound.
A program may use at most 64 MiB of HBM per device.

```python
import math
import jax
import jax.numpy as jnp
import numpy as np
from jax import lax

D = 8192
FF = 28672
RANK = 64
BLK = 128
STEPS = 2
NBLK = 2
ROWS = 256
NADP = 64


def touch_ends(array, rng, smallest, top_value):
    place = [jax.random.randint(jax.random.fold_in(rng, axis), (), 0, length) for axis, length in enumerate(array.shape)]
    longest = array.shape.index(max(array.shape))
    neighbour = place[:longest] + [(place[longest] + 1) % array.shape[longest]] + place[longest + 1:]
    return array.at[tuple(place)].set(smallest).at[tuple(neighbour)].set(top_value)


def block_levels(key, dims, split, low, top_value):
    def one(dim, parts):
        steps = jax.random.uniform(jax.random.fold_in(jax.random.fold_in(key, 6), dim), (parts,), jnp.float32, low / len(split), top_value / len(split))
        return jnp.repeat(jnp.exp(steps), dims[dim] // parts).reshape((-1,) + (1,) * (len(dims) - dim - 1))

    factor_of = one(*split[0])
    for cut in split[1:]:
        factor_of = factor_of * one(*cut)
    return factor_of


def rank_table(amount, skew):
    weights = [(1 << 20) // math.isqrt(standing ** skew) + 1 for standing in range(1, amount + 1)]
    scale = 1 + sum(weights) // (1 << 30)
    return np.cumsum(np.array([max(1, weight // scale) for weight in weights]))


def skewed_ids(rng, extent, amount, lean):
    grid = rank_table(amount, lean)
    pick = jax.random.randint(jax.random.fold_in(rng, 1), extent, 0, int(grid[amount - 1]))
    standing = jnp.searchsorted(jnp.asarray(grid, jnp.int32), pick, side="right")
    return jax.random.permutation(jax.random.fold_in(rng, 2), amount)[standing].astype(jnp.int32)


def profile(number_of, total, bound, lean):
    loads = [(1 << 20) // math.isqrt(grade ** lean) + 1 for grade in range(2, number_of + 1)]
    rest, holding = total - bound - (number_of - 1), [1] * (number_of - 1)
    while rest > 0:
        movable = [i for i in range(number_of - 1) if holding[i] < bound]
        whole, remaining = sum([loads[i] for i in movable]), rest
        for i in movable:
            more = min(bound - holding[i], max(1, remaining * loads[i] // whole), rest)
            holding[i] = holding[i] + more
            rest = rest - more
    return np.array([bound] + holding)


def ragged(stream_key, number_of, total, bound, slope):
    if number_of == 2:
        one = jax.random.randint(stream_key, (), max(1, total - bound), min(bound, total - 1) + 1)
        return jnp.stack([one, total - one])
    lengths = jnp.asarray(profile(number_of, total, bound, slope), jnp.int32)
    twos = (number_of - 1) // 2
    donor, taker = lengths[1:1 + 2 * twos:2], lengths[2:2 + 2 * twos:2]
    slack = jnp.minimum(donor - 1, bound - taker)
    passed = jax.random.randint(jax.random.fold_in(stream_key, 1), (twos,), 0, 1 << 20) % (slack + 1)
    lengths = lengths.at[1:1 + 2 * twos:2].set(donor - passed).at[2:2 + 2 * twos:2].set(taker + passed)
    return lengths[jax.random.permutation(jax.random.fold_in(stream_key, 2), number_of)]


def scatter_about(rng, shape, scale, bound, cuts=(), held_as=jnp.bfloat16):
    array = jax.random.normal(rng, shape, jnp.float32) * scale
    if len(cuts) > 0:
        array = block_levels(rng, shape, cuts, -0.22, 0.18) * array
    return jnp.clip(array, min=-bound, max=bound).astype(held_as)


def setup_inputs(seed: int = 0) -> dict:
    keys = jax.random.split(jax.random.key(seed), 9)
    return {
        "tokens": scatter_about(keys[0], (STEPS, ROWS, D), 1.0, 6.0, ((2, 8),)),
        "gate_up_weight": scatter_about(keys[1], (D, 2, FF), D ** -0.5, 0.0625, ((0, 8), (2, 64))),
        "down_weight": scatter_about(keys[2], (FF, D), FF ** -0.5, 0.03125, ((0, 64), (1, 8))),
        "shrink_store": scatter_about(keys[3], (NADP, 2, D, RANK), D ** -0.5, 0.0625, ((0, 64), (2, 8))),
        "expand_store": scatter_about(keys[4], (NADP, 2, RANK, FF), RANK ** -0.5, 0.75, ((0, 64), (2, 8))),
        "block_adapter": touch_ends(skewed_ids(keys[5], (STEPS, NBLK), NADP, 2), jax.random.fold_in(keys[5], 3), 0, NADP - 1).astype(jnp.int32),
        "block_live": jax.vmap(lambda own: ragged(own, NBLK, BLK + (NBLK - 1) * BLK // 2, BLK, 0))(jax.random.split(keys[6], STEPS)).reshape((STEPS, NBLK)).astype(jnp.int32),
        "adapter_slot": jax.random.permutation(keys[7], NADP).astype(jnp.int32),
    }


def reference(tokens, gate_up_weight, down_weight, shrink_store, expand_store, block_adapter, block_live, adapter_slot):
    highest = lax.Precision.HIGHEST
    flat_weight = gate_up_weight.reshape(D, 2 * FF)
    row_index = jnp.arange(ROWS)
    outputs = []
    for decode_step in range(STEPS):
        inputs = tokens[decode_step]
        pieces = []
        for block_index in range(NBLK):
            slot = adapter_slot[block_adapter[decode_step, block_index]]
            first = shrink_store[slot].astype(jnp.float32)
            second = expand_store[slot].astype(jnp.float32)
            block_rows = inputs[block_index * BLK:(block_index + 1) * BLK].astype(jnp.float32)
            shrunk = jnp.einsum("nd,kdc->knc", block_rows, first, precision=highest)
            pieces.append(jnp.einsum("knc,kcf->nkf", shrunk, second, precision=highest))
        adapted = jnp.concatenate(pieces, axis=0)
        gate_up = jnp.dot(inputs, flat_weight, preferred_element_type=jnp.float32).reshape(ROWS, 2, FF) + adapted
        hidden = (jax.nn.silu(gate_up[:, 0]) * gate_up[:, 1]).astype(jnp.bfloat16)
        owners = row_index // BLK
        live = jnp.sum((owners[:, None] == jnp.arange(NBLK)[None, :]) * block_live[decode_step][None, :], axis=1)
        keep = ((row_index % BLK) < live).astype(jnp.float32)
        summed = jnp.dot(hidden, down_weight, preferred_element_type=jnp.float32)
        outputs.append((summed * keep[:, None]).astype(jnp.bfloat16))
    return jnp.stack(outputs)
```

```python
import functools

import jax
import jax.numpy as jnp
from jax import lax
from jax.experimental import pallas as pl
from jax.experimental.pallas import tpu as pltpu
from jax.sharding import PartitionSpec as P

NBLK = 2
STEPS = 2
NSB = STEPS * NBLK
WIN = 512
MESH = pl.DeviceIdType.MESH
F32 = jnp.float32
BF16 = jnp.bfloat16


class Exchange:
    def __init__(self, ssem, rsem, phase, n, me, dev):
        self.ssem, self.rsem, self.phase = ssem, rsem, phase
        self.n, self.me, self.dev = n, me, dev

    def copy(self, k, src, dst, source):
        peer = lax.rem(self.me + k, self.n)
        return pltpu.make_async_remote_copy(
            src_ref=src(peer),
            dst_ref=dst(source),
            send_sem=self.ssem.at[self.phase, k],
            recv_sem=self.rsem.at[self.phase, source],
            device_id=self.dev(peer),
            device_id_type=MESH,
        )

    def start(self, src, dst):
        self.src, self.dst = src, dst
        for k in range(1, self.n):
            self.copy(k, src, dst, self.me).start()

    def wait_recv(self):
        for k in range(1, self.n):
            self.copy(k, self.src, self.dst, lax.rem(self.me + k, self.n)).wait_recv()

    def wait_send(self):
        for k in range(1, self.n):
            self.copy(k, self.src, self.dst, self.me).wait_send()


def nt(a, b):
    return lax.dot_general(a, b, (((1,), (1,)), ((), ())), preferred_element_type=F32)


def kernel(
    ny, nz, block,
    adapter_ref, live_ref, slot_ref, tok_h, w_h, s_h, e_h, d_h, out_ref,
    tok, w, sh, ev, dn,
    sp, srx, sy, sz, pb, brx,
    e1y, e1z, sel0, sel1, e2y, e2z, ets, erx, ecat,
    hid, o0, o1, r0, r1, acc0, acc1, q0, q1, u0, u1,
    ssem, rsem, lsem,
):
    nt_ = lax.axis_size("tensor")
    p = lax.axis_index("pool")
    t = lax.axis_index("tensor")
    y = lax.div(p, nz)
    z = lax.rem(p, nz)
    rows_t = tok.shape[0] // nt_
    ranks = s_h.shape[1]
    units = w_h.shape[1]
    step_rows = tok.shape[0] // STEPS
    grp = step_rows // (ny * nz)
    span = nz * units
    zshift = nz.bit_length() - 1

    def ydev(i):
        return (i * nz + z, t)

    def zdev(i):
        return (y * nz + i, t)

    def tdev(i):
        return (p, i)

    def win(zi):
        return pl.multiple_of(lax.div(zi * units, 128) * 128, 128)

    barrier = pltpu.get_barrier_semaphore()
    for n, me, dev in ((ny, y, ydev), (nz, z, zdev), (nt_, t, tdev)):
        for k in range(1, n):
            pl.semaphore_signal(
                barrier, inc=1, device_id=dev(lax.rem(me + k, n)), device_id_type=MESH
            )

    loads = [
        pltpu.make_async_copy(s_h.at[0], sh.at[pl.ds(0, ranks)], lsem.at[0]),
        pltpu.make_async_copy(s_h.at[1], sh.at[pl.ds(ranks, ranks)], lsem.at[1]),
        pltpu.make_async_copy(tok_h, tok, lsem.at[2]),
        pltpu.make_async_copy(w_h, w, lsem.at[3]),
        pltpu.make_async_copy(d_h, dn, lsem.at[4]),
        pltpu.make_async_copy(
            e_h.at[0, :, pl.ds(pl.multiple_of(y * span, 128), span)], e1y.at[y], lsem.at[5]
        ),
    ]
    ecopies = [
        pltpu.make_async_copy(
            e_h.at[1, :, pl.ds(i * span, span)], ev.at[i], lsem.at[6 + i]
        )
        for i in range(ny)
    ]
    for c in ecopies + loads:
        c.start()

    exch = functools.partial(Exchange, ssem, rsem)
    x_e1y = exch(0, ny, y, ydev)
    x_e1z = exch(1, nz, z, zdev)
    x_s = exch(2, nt_, t, tdev)
    x_b = [exch(3, nt_, t, tdev), exch(4, nt_, t, tdev)]
    x_sy = exch(5, ny, y, ydev)
    x_sz = exch(6, nz, z, zdev)
    x_e2y = exch(7, nz, z, zdev)
    x_e2z = exch(8, ny, y, ydev)
    x_et = exch(9, nt_, t, tdev)
    x_h = exch(10, nt_, t, tdev)
    x_o0 = exch(11, ny, y, ydev)
    x_o1 = exch(12, nz, z, zdev)
    x_q0 = exch(13, nz, z, zdev)
    x_q1 = exch(14, ny, y, ydev)

    for c in ecopies:
        c.wait()
    pl.semaphore_wait(barrier, (ny - 1) + (nz - 1) + (nt_ - 1))

    x_e1y.start(
        lambda i: e_h.at[0, :, pl.ds(pl.multiple_of(i * span, 128), span)],
        lambda m: e1y.at[m],
    )
    x_e1z.start(lambda i: ev.at[:, :, pl.ds(win(i), WIN)], lambda m: e1z.at[m])
    own_z = pltpu.make_async_copy(
        ev.at[:, :, pl.ds(win(z), WIN)], e1z.at[z], lsem.at[6 + ny]
    )
    own_z.start()

    for c in loads[:3]:
        c.wait()
    s_part = nt(tok[...], sh[...]).astype(BF16)
    for i in range(nt_):
        sp[i] = s_part[i * rows_t:(i + 1) * rows_t]
    x_s.start(lambda i: sp.at[i], lambda m: srx.at[m])

    loads[3].wait()

    def base(k):
        part = nt(tok[...], w[k]).astype(BF16)
        for i in range(nt_):
            pb[k, i] = part[i * rows_t:(i + 1) * rows_t]
        x_b[k].start(lambda i: pb.at[k, i], lambda m: brx.at[k, m])

    base(0)

    x_s.wait_recv()
    total = sp[t].astype(F32)
    for k in range(1, nt_):
        total = total + srx[lax.rem(t + k, nt_)].astype(F32)
    sy[y] = total.astype(BF16)
    x_sy.start(lambda i: sy.at[y], lambda m: sy.at[m])

    base(1)

    slots = [slot_ref[adapter_ref[i // NBLK, i % NBLK]] for i in range(NSB)]
    yo = [lax.shift_right_logical(s, zshift) for s in slots]
    zo = [lax.bitwise_and(s, nz - 1) for s in slots]
    mine = lax.div(t * rows_t, block)
    my_slot = slot_ref[adapter_ref[lax.div(mine, NBLK), lax.rem(mine, NBLK)]]
    my_yo = lax.shift_right_logical(my_slot, zshift)
    my_zo = lax.bitwise_and(my_slot, nz - 1)

    x_sy.wait_recv()
    sz[z] = sy[my_yo]
    x_sz.start(lambda i: sz.at[z], lambda m: sz.at[m])

    loads[5].wait()
    x_e1y.wait_recv()
    for i in range(NSB):
        sel0[i] = e1y[yo[i]]
    x_e2y.start(lambda i: sel0.at[:, :, pl.ds(win(i), WIN)], lambda m: e2y.at[m])
    e2y[z] = sel0[:, :, pl.ds(win(z), WIN)]
    own_z.wait()
    x_e1z.wait_recv()
    for i in range(NSB):
        sel1[i] = e1z[zo[i]]
    x_e2z.start(lambda i: sel1.at[:, i], lambda m: e2z.at[m])
    e2z[y] = sel1[:, y]

    sums = []
    for k in range(2):
        x_b[k].wait_recv()
        total = pb[k, t].astype(F32)
        for j in range(1, nt_):
            total = total + brx[k, lax.rem(t + j, nt_)].astype(F32)
        sums.append(total)

    x_sz.wait_recv()
    shrunk = sz[my_zo]

    x_e2y.wait_recv()
    for i in range(NSB):
        ets[i, 0] = e2y[zo[i], i]
    x_e2z.wait_recv()
    for i in range(NSB):
        ets[i, 1] = e2z[yo[i], i]
    x_et.start(lambda i: ets.at[lax.div(i * rows_t, block)], lambda m: erx.at[m])
    erx[t] = ets[mine]
    x_et.wait_recv()
    rank_t = ranks // nt_
    for k in range(2):
        for i in range(nt_):
            ecat[pl.ds(k * ranks + i * rank_t, rank_t)] = erx[i, k].astype(F32)
    second = ecat[...]
    rolled = pltpu.roll(second, WIN - 64, axis=1)
    odd = lax.rem(z, 2) == 1
    second = jnp.where(odd, rolled, second).astype(BF16)
    lane = lax.broadcasted_iota(jnp.int32, shrunk.shape, 1)
    zero = jnp.zeros_like(shrunk)
    gate = jnp.dot(jnp.where(lane < ranks, shrunk, zero), second, preferred_element_type=F32)
    up = jnp.dot(jnp.where(lane < ranks, zero, shrunk), second, preferred_element_type=F32)
    gate = sums[0] + gate[:, :units]
    up = sums[1] + up[:, :units]
    hid[t] = (gate / (1.0 + jnp.exp(-gate)) * up).astype(BF16)
    x_h.start(lambda i: hid.at[t], lambda m: hid.at[m])
    loads[4].wait()
    x_h.wait_recv()

    half = nt_ // STEPS
    h0 = hid[0:half].reshape(step_rows, units)
    part = jnp.dot(h0, dn[...], preferred_element_type=F32).astype(BF16)
    for i in range(ny):
        o0[i] = part[i * nz * grp:(i + 1) * nz * grp]
    x_o0.start(lambda i: o0.at[i], lambda m: r0.at[m])

    h1 = hid[half:nt_].reshape(step_rows, units)
    ri = lax.broadcasted_iota(jnp.int32, (step_rows, step_rows), 0)
    ci = lax.broadcasted_iota(jnp.int32, (step_rows, step_rows), 1)
    gbits = grp.bit_length() - 1
    ybits = ny.bit_length() - 1
    low = lax.bitwise_and(ri, grp - 1)
    yy = lax.bitwise_and(lax.shift_right_logical(ri, gbits), ny - 1)
    zz = lax.shift_right_logical(ri, gbits + ybits)
    perm = jnp.where(ci == yy * (nz * grp) + zz * grp + low, 1.0, 0.0).astype(BF16)
    h1 = jnp.dot(perm, h1, preferred_element_type=F32).astype(BF16)
    part = jnp.dot(h1, dn[...], preferred_element_type=F32).astype(BF16)
    for i in range(nz):
        o1[i] = part[i * ny * grp:(i + 1) * ny * grp]
    x_o1.start(lambda i: o1.at[i], lambda m: r1.at[m])

    x_o0.wait_recv()
    total = o0[y].astype(F32)
    for k in range(1, ny):
        total = total + r0[lax.rem(y + k, ny)].astype(F32)
    acc0[...] = total
    for i in range(nz):
        q0[i] = acc0[pl.ds(i * grp, grp), :]
    x_q0.start(lambda i: q0.at[i], lambda m: u0.at[m])

    x_o1.wait_recv()
    total = o1[z].astype(F32)
    for k in range(1, nz):
        total = total + r1[lax.rem(z + k, nz)].astype(F32)
    acc1[...] = total
    for i in range(ny):
        q1[i] = acc1[pl.ds(i * grp, grp), :]
    x_q1.start(lambda i: q1.at[i], lambda m: u1.at[m])

    first = p * grp
    place = lax.rem(first, block) + lax.broadcasted_iota(jnp.int32, q0.shape[1:], 0)
    owner = lax.div(first, block)
    for step, (x, q, u, n, me) in enumerate(
        ((x_q0, q0, u0, nz, z), (x_q1, q1, u1, ny, y))
    ):
        x.wait_recv()
        total = q[me]
        for k in range(1, n):
            total = total + u[lax.rem(me + k, n)]
        keep = place < live_ref[step, owner]
        out_ref[step] = jnp.where(keep, total, 0.0).astype(BF16)

    for x in (x_e1y, x_e1z, x_s, *x_b, x_sy, x_sz, x_e2y, x_e2z, x_et, x_h,
              x_o0, x_o1, x_q0, x_q1):
        x.wait_send()


def shards(ny, nz, block, tokens, gate_up, down, shrink, expand, adapter, live, slots):
    steps, rows, width = tokens.shape
    units = gate_up.shape[2]
    ranks = shrink.shape[3]
    rank_t = expand.shape[2]
    n_t = lax.axis_size("tensor")
    rows_t = steps * rows // n_t
    grp = rows // (ny * nz)
    span = nz * units
    any_spec = pl.BlockSpec(memory_space=pl.ANY)
    smem = pl.BlockSpec(memory_space=pltpu.SMEM)
    vmem = pltpu.VMEM
    scratch = [
        vmem((steps * rows, width), BF16),
        vmem((2, units, width), BF16),
        vmem((2 * ranks, width), BF16),
        vmem((ny, rank_t, span), BF16),
        vmem((units, width), BF16),
        vmem((n_t, rows_t, 2 * ranks), BF16),
        vmem((n_t, rows_t, 2 * ranks), BF16),
        vmem((ny, rows_t, 2 * ranks), BF16),
        vmem((nz, rows_t, 2 * ranks), BF16),
        vmem((2, n_t, rows_t, units), BF16),
        vmem((2, n_t, rows_t, units), BF16),
        vmem((ny, rank_t, span), BF16),
        vmem((nz, ny, rank_t, WIN), BF16),
        vmem((NSB, rank_t, span), BF16),
        vmem((NSB, ny, rank_t, WIN), BF16),
        vmem((nz, NSB, rank_t, WIN), BF16),
        vmem((ny, NSB, rank_t, WIN), BF16),
        vmem((NSB, 2, rank_t, WIN), BF16),
        vmem((n_t, 2, rank_t, WIN), BF16),
        vmem((2 * ranks, WIN), F32),
        vmem((n_t, rows_t, units), BF16),
        vmem((ny, nz * grp, width), BF16),
        vmem((nz, ny * grp, width), BF16),
        vmem((ny, nz * grp, width), BF16),
        vmem((nz, ny * grp, width), BF16),
        vmem((nz * grp, width), F32),
        vmem((ny * grp, width), F32),
        vmem((nz, grp, width), F32),
        vmem((ny, grp, width), F32),
        vmem((nz, grp, width), F32),
        vmem((ny, grp, width), F32),
        pltpu.SemaphoreType.DMA((15, max(ny, nz, n_t))),
        pltpu.SemaphoreType.DMA((15, max(ny, nz, n_t))),
        pltpu.SemaphoreType.DMA((7 + ny,)),
    ]
    return pl.pallas_call(
        functools.partial(kernel, ny, nz, block),
        out_shape=jax.ShapeDtypeStruct((steps, grp, width), BF16),
        in_specs=[smem, smem, smem] + [any_spec] * 5,
        out_specs=pl.BlockSpec(memory_space=pltpu.VMEM),
        scratch_shapes=scratch,
        compiler_params=pltpu.CompilerParams(collective_id=0, has_side_effects=True),
        name="layer",
    )(
        adapter,
        live,
        slots,
        tokens.reshape(steps * rows, width),
        gate_up.transpose(1, 2, 0),
        shrink[0].transpose(0, 2, 1),
        expand[0],
        down,
    )


def build(mesh, ny, nz, block):
    return jax.shard_map(
        functools.partial(shards, ny, nz, block),
        mesh=mesh,
        in_specs=(
            P(None, None, "tensor"),
            P("tensor", None, "pool"),
            P("pool", "tensor"),
            P("pool", None, "tensor", None),
            P("pool", None, "tensor", None),
            P(),
            P(),
            P(),
        ),
        out_specs=P(None, "pool", "tensor"),
        check_vma=False,
    )


def solution(mesh):
    return build(mesh, 8, 8, 128)
```

```python
import functools

import jax
import jax.numpy as jnp
from jax import lax
from jax.experimental import pallas as pl
from jax.experimental.pallas import tpu as pltpu
from jax.sharding import PartitionSpec as P

NBLK = 2
STEPS = 2
NSB = STEPS * NBLK
CORES = 2
WIN = 512
MESH = pl.DeviceIdType.MESH
F32 = jnp.float32
BF16 = jnp.bfloat16


class Exchange:
    def __init__(self, ssem, rsem, phase, me, peers, dev):
        self.ssem, self.rsem, self.phase = ssem, rsem, phase
        self.me, self.peers, self.dev = me, peers, dev

    def copy(self, peer, src, dst, source):
        return pltpu.make_async_remote_copy(
            src_ref=src(peer),
            dst_ref=dst(source),
            send_sem=self.ssem.at[self.phase, peer],
            recv_sem=self.rsem.at[self.phase, source],
            device_id=self.dev(peer),
            device_id_type=MESH,
        )

    def start(self, src, dst):
        self.src, self.dst = src, dst
        for peer in self.peers:
            self.copy(peer, src, dst, self.me).start()

    def wait_from(self, peer):
        self.copy(peer, self.src, self.dst, peer).wait_recv()

    def wait_recv(self):
        for peer in self.peers:
            self.wait_from(peer)

    def wait_send(self):
        for peer in self.peers:
            self.copy(peer, self.src, self.dst, self.me).wait_send()


def nt(a, b):
    return lax.dot_general(a, b, (((1,), (1,)), ((), ())), preferred_element_type=F32)


def kernel(
    ny, nz, block,
    adapter_ref, live_ref, slot_ref, tok_h, w_h, s_h, e_h, d_h, out_ref,
    tok, w, sh, ev, dn,
    sp, srx, sy, sz, pb, brx,
    e1y, e1z, sel0, sel1, e2y, e2z, ets, erx, ecat,
    hid, o0, o1, r0, r1, acc0, acc1, q0, q1, u0, u1,
    ssem, rsem, lsem, os0, or0, os1, or1,
):
    nt_ = lax.axis_size("tensor")
    p = lax.axis_index("pool")
    t = lax.axis_index("tensor")
    y = lax.div(p, nz)
    z = lax.rem(p, nz)
    rows_t = tok.shape[0] // nt_
    ranks = s_h.shape[1]
    units = w_h.shape[1]
    step_rows = tok.shape[0] // STEPS
    grp = step_rows // (ny * nz)
    span = nz * units
    zshift = nz.bit_length() - 1

    nx = nt_ // CORES
    x = lax.div(t, CORES)
    core = lax.rem(t, CORES)
    width = dn.shape[1]
    hw = width // 2
    hops = [0] + sorted(range(1, nx), key=lambda d: min(d, nx - d))
    chips = [lax.rem(x + d, nx) for d in hops]
    ypeers = [lax.rem(y + k, ny) for k in range(1, ny)]
    zpeers = [lax.rem(z + k, nz) for k in range(1, nz)]
    other = CORES * x + (CORES - 1 - core)
    tpeers = [other] + [
        CORES * c + lax.rem(core + i, CORES) for c in chips[1:] for i in range(CORES)
    ]

    def ydev(i):
        return (i * nz + z, t)

    def zdev(i):
        return (y * nz + i, t)

    def tdev(i):
        return (p, i)

    def win(zi):
        return pl.multiple_of(lax.div(zi * units, 128) * 128, 128)

    barrier = pltpu.get_barrier_semaphore()
    for peers, dev in ((ypeers, ydev), (zpeers, zdev), (tpeers, tdev)):
        for i in peers:
            pl.semaphore_signal(barrier, inc=1, device_id=dev(i), device_id_type=MESH)

    loads = [
        pltpu.make_async_copy(s_h.at[0], sh.at[pl.ds(0, ranks)], lsem.at[0]),
        pltpu.make_async_copy(s_h.at[1], sh.at[pl.ds(ranks, ranks)], lsem.at[1]),
        pltpu.make_async_copy(tok_h, tok, lsem.at[2]),
        pltpu.make_async_copy(w_h, w, lsem.at[3]),
        pltpu.make_async_copy(d_h, dn, lsem.at[4]),
        pltpu.make_async_copy(
            e_h.at[0, :, pl.ds(pl.multiple_of(y * span, 128), span)], e1y.at[y], lsem.at[5]
        ),
    ]
    ecopies = [
        pltpu.make_async_copy(
            e_h.at[1, :, pl.ds(i * span, span)], ev.at[i], lsem.at[6 + i]
        )
        for i in range(ny)
    ]
    for c in ecopies + loads:
        c.start()

    def on_y(phase):
        return Exchange(ssem, rsem, phase, y, ypeers, ydev)

    def on_z(phase):
        return Exchange(ssem, rsem, phase, z, zpeers, zdev)

    def on_t(phase):
        return Exchange(ssem, rsem, phase, t, tpeers, tdev)

    x_e1y, x_e1z = on_y(0), on_z(1)
    x_s, x_sy, x_sz = on_t(2), on_y(3), on_z(4)
    x_b = [on_t(5), on_t(6)]
    x_e2y, x_e2z, x_et = on_z(7), on_y(8), on_t(9)
    x_h = on_t(10)
    x_q0, x_q1 = on_z(11), on_y(12)

    for c in ecopies:
        c.wait()
    pl.semaphore_wait(barrier, (ny - 1) + (nz - 1) + (nt_ - 1))

    x_e1y.start(
        lambda i: e_h.at[0, :, pl.ds(pl.multiple_of(i * span, 128), span)],
        lambda m: e1y.at[m],
    )
    x_e1z.start(lambda i: ev.at[:, :, pl.ds(win(i), WIN)], lambda m: e1z.at[m])
    own_z = pltpu.make_async_copy(
        ev.at[:, :, pl.ds(win(z), WIN)], e1z.at[z], lsem.at[6 + ny]
    )
    own_z.start()

    for c in loads[:3]:
        c.wait()
    s_part = nt(tok[...], sh[...])
    for i in range(nt_):
        sp[i] = s_part[i * rows_t:(i + 1) * rows_t]
    x_s.start(lambda i: sp.at[i], lambda m: srx.at[m])

    loads[3].wait()

    def base(k):
        part = nt(tok[...], w[k]).astype(BF16)
        for i in range(nt_):
            pb[k, i] = part[i * rows_t:(i + 1) * rows_t]
        x_b[k].start(lambda i: pb.at[k, i], lambda m: brx.at[k, m])

    base(0)

    x_s.wait_recv()
    total = sp[t]
    for i in tpeers:
        total = total + srx[i]
    sy[y] = total.astype(BF16)
    x_sy.start(lambda i: sy.at[y], lambda m: sy.at[m])

    base(1)

    slots = [slot_ref[adapter_ref[i // NBLK, i % NBLK]] for i in range(NSB)]
    yo = [lax.shift_right_logical(s, zshift) for s in slots]
    zo = [lax.bitwise_and(s, nz - 1) for s in slots]
    mine = lax.div(t * rows_t, block)
    my_slot = slot_ref[adapter_ref[lax.div(mine, NBLK), lax.rem(mine, NBLK)]]
    my_yo = lax.shift_right_logical(my_slot, zshift)
    my_zo = lax.bitwise_and(my_slot, nz - 1)

    loads[5].wait()
    x_e1y.wait_recv()
    for i in range(NSB):
        sel0[i] = e1y[yo[i]]
    x_e2y.start(lambda i: sel0.at[:, :, pl.ds(win(i), WIN)], lambda m: e2y.at[m])
    own_z.wait()
    x_e1z.wait_recv()
    for i in range(NSB):
        sel1[i] = e1z[zo[i]]
    x_e2z.start(lambda i: sel1.at[:, i], lambda m: e2z.at[m])
    x_sy.wait_recv()
    sz[z] = sy[my_yo]
    x_sz.start(lambda i: sz.at[z], lambda m: sz.at[m])
    e2y[z] = sel0[:, :, pl.ds(win(z), WIN)]
    e2z[y] = sel1[:, y]

    sums = []
    for k in range(2):
        x_b[k].wait_recv()
        total = pb[k, t].astype(F32)
        for i in tpeers:
            total = total + brx[k, i].astype(F32)
        sums.append(total)

    x_e2y.wait_recv()
    for i in range(NSB):
        ets[i, 0] = e2y[zo[i], i]
    x_e2z.wait_recv()
    for i in range(NSB):
        ets[i, 1] = e2z[yo[i], i]
    x_et.start(lambda i: ets.at[lax.div(i * rows_t, block)], lambda m: erx.at[m])
    erx[t] = ets[mine]
    x_sz.wait_recv()
    shrunk = sz[my_zo]
    x_et.wait_recv()
    rank_t = ranks // nt_
    for k in range(2):
        for i in range(nt_):
            ecat[pl.ds(k * ranks + i * rank_t, rank_t)] = erx[i, k].astype(F32)
    second = ecat[...]
    rolled = pltpu.roll(second, WIN - 64, axis=1)
    odd = lax.rem(z, 2) == 1
    second = jnp.where(odd, rolled, second).astype(BF16)
    lane = lax.broadcasted_iota(jnp.int32, shrunk.shape, 1)
    zero = jnp.zeros_like(shrunk)
    gate = jnp.dot(jnp.where(lane < ranks, shrunk, zero), second, preferred_element_type=F32)
    up = jnp.dot(jnp.where(lane < ranks, zero, shrunk), second, preferred_element_type=F32)
    gate = sums[0] + gate[:, :units]
    up = sums[1] + up[:, :units]
    hid[t] = (gate / (1.0 + jnp.exp(-gate)) * up).astype(BF16)
    x_h.start(lambda i: hid.at[t], lambda m: hid.at[m])
    loads[4].wait()

    gps = nx // STEPS
    ypg = ny // gps
    rows_g = CORES * rows_t
    part_y = nz * grp
    part_z = ypg * grp
    ri = lax.broadcasted_iota(jnp.int32, (rows_g, rows_g), 0)
    ci = lax.broadcasted_iota(jnp.int32, (rows_g, rows_g), 1)
    gbits = grp.bit_length() - 1
    ybits = ypg.bit_length() - 1
    low = lax.bitwise_and(ri, grp - 1)
    yy = lax.bitwise_and(lax.shift_right_logical(ri, gbits), ypg - 1)
    zz = lax.shift_right_logical(ri, gbits + ybits)
    perm = jnp.where(ci == yy * part_y + zz * grp + low, 1.0, 0.0).astype(BF16)

    def copy_y(peer, source, step):
        return pltpu.make_async_remote_copy(
            src_ref=o0.at[peer, step],
            dst_ref=r0.at[source, step],
            send_sem=os0.at[peer, step],
            recv_sem=or0.at[source, step],
            device_id=ydev(peer),
            device_id_type=MESH,
        )

    def copy_z(peer, source, chip):
        return pltpu.make_async_remote_copy(
            src_ref=o1.at[peer, chip],
            dst_ref=r1.at[source, chip],
            send_sem=os1.at[peer, chip],
            recv_sem=or1.at[source, chip],
            device_id=zdev(peer),
            device_id_type=MESH,
        )

    for j, chip in enumerate(chips):
        for i in tpeers[:1] if j == 0 else tpeers[CORES * j - 1:CORES * j + 1]:
            x_h.wait_from(i)
        h = hid[pl.ds(CORES * chip, CORES)].reshape(rows_g, units)
        step = lax.div(chip, gps)
        first = lax.rem(chip, gps) * ypg
        part = jnp.dot(h, dn[:, :hw], preferred_element_type=F32).astype(BF16)
        for i in range(ypg):
            o0[first + i, step] = part[i * part_y:(i + 1) * part_y]
        for i in range(ypg):
            peer = first + lax.rem(y + i, ypg)

            @pl.when(peer != y)
            def _(peer=peer, step=step):
                copy_y(peer, y, step).start()

        h = jnp.dot(perm, h, preferred_element_type=F32).astype(BF16)
        part = jnp.dot(h, dn[:, hw:], preferred_element_type=F32).astype(BF16)
        for i in range(nz):
            o1[i, chip] = part[i * part_z:(i + 1) * part_z]
        for peer in zpeers:
            copy_z(peer, z, chip).start()

    total = o0[y].astype(F32)
    for i in ypeers:
        for step in range(STEPS):
            copy_y(i, i, step).wait_recv()
        total = total + r0[i].astype(F32)
    acc0[...] = total
    for i in range(nz):
        q0[i] = acc0[:, pl.ds(i * grp, grp), :]
    x_q0.start(lambda i: q0.at[i], lambda m: u0.at[m])

    total = o1[z].astype(F32)
    for i in zpeers:
        for chip in range(nx):
            copy_z(i, i, chip).wait_recv()
        total = total + r1[i].astype(F32)
    acc1[...] = total.reshape(STEPS, ny * grp, hw)
    for i in range(ny):
        q1[i] = acc1[:, pl.ds(i * grp, grp), :]
    x_q1.start(lambda i: q1.at[i], lambda m: u1.at[m])

    first = p * grp
    place = lax.rem(first, block) + lax.broadcasted_iota(jnp.int32, (grp, hw), 0)
    owner = lax.div(first, block)
    for half, (xq, q, u, peers, me) in enumerate(
        ((x_q0, q0, u0, zpeers, z), (x_q1, q1, u1, ypeers, y))
    ):
        total = q[me]
        for i in peers:
            xq.wait_from(i)
            total = total + u[i]
        for step in range(STEPS):
            keep = place < live_ref[step, owner]
            out_ref[step, :, half * hw:(half + 1) * hw] = jnp.where(
                keep, total[step], 0.0
            ).astype(BF16)

    for e in (x_e1y, x_e1z, x_s, *x_b, x_sy, x_sz, x_e2y, x_e2z, x_et, x_h, x_q0, x_q1):
        e.wait_send()
    for i in ypeers:
        for step in range(STEPS):
            copy_y(i, y, step).wait_send()
    for i in zpeers:
        for chip in range(nx):
            copy_z(i, z, chip).wait_send()


def shards(ny, nz, block, tokens, gate_up, down, shrink, expand, adapter, live, slots):
    steps, rows, width = tokens.shape
    units = gate_up.shape[2]
    ranks = shrink.shape[3]
    rank_t = expand.shape[2]
    n_t = lax.axis_size("tensor")
    rows_t = steps * rows // n_t
    grp = rows // (ny * nz)
    span = nz * units
    hw = width // 2
    nx = n_t // CORES
    part_z = ny // (nx // steps) * grp
    any_spec = pl.BlockSpec(memory_space=pl.ANY)
    smem = pl.BlockSpec(memory_space=pltpu.SMEM)
    vmem = pltpu.VMEM
    scratch = [
        vmem((steps * rows, width), BF16),
        vmem((2, units, width), BF16),
        vmem((2 * ranks, width), BF16),
        vmem((ny, rank_t, span), BF16),
        vmem((units, width), BF16),
        vmem((n_t, rows_t, 2 * ranks), F32),
        vmem((n_t, rows_t, 2 * ranks), F32),
        vmem((ny, rows_t, 2 * ranks), BF16),
        vmem((nz, rows_t, 2 * ranks), BF16),
        vmem((2, n_t, rows_t, units), BF16),
        vmem((2, n_t, rows_t, units), BF16),
        vmem((ny, rank_t, span), BF16),
        vmem((nz, ny, rank_t, WIN), BF16),
        vmem((NSB, rank_t, span), BF16),
        vmem((NSB, ny, rank_t, WIN), BF16),
        vmem((nz, NSB, rank_t, WIN), BF16),
        vmem((ny, NSB, rank_t, WIN), BF16),
        vmem((NSB, 2, rank_t, WIN), BF16),
        vmem((n_t, 2, rank_t, WIN), BF16),
        vmem((2 * ranks, WIN), F32),
        vmem((n_t, rows_t, units), BF16),
        vmem((ny, steps, nz * grp, hw), BF16),
        vmem((nz, nx, part_z, hw), BF16),
        vmem((ny, steps, nz * grp, hw), BF16),
        vmem((nz, nx, part_z, hw), BF16),
        vmem((steps, nz * grp, hw), F32),
        vmem((steps, ny * grp, hw), F32),
        vmem((nz, steps, grp, hw), F32),
        vmem((ny, steps, grp, hw), F32),
        vmem((nz, steps, grp, hw), F32),
        vmem((ny, steps, grp, hw), F32),
        pltpu.SemaphoreType.DMA((13, max(ny, nz, n_t))),
        pltpu.SemaphoreType.DMA((13, max(ny, nz, n_t))),
        pltpu.SemaphoreType.DMA((7 + ny,)),
        pltpu.SemaphoreType.DMA((ny, steps)),
        pltpu.SemaphoreType.DMA((ny, steps)),
        pltpu.SemaphoreType.DMA((nz, nx)),
        pltpu.SemaphoreType.DMA((nz, nx)),
    ]
    return pl.pallas_call(
        functools.partial(kernel, ny, nz, block),
        out_shape=jax.ShapeDtypeStruct((steps, grp, width), BF16),
        in_specs=[smem, smem, smem] + [any_spec] * 5,
        out_specs=pl.BlockSpec(memory_space=pltpu.VMEM),
        scratch_shapes=scratch,
        compiler_params=pltpu.CompilerParams(collective_id=0, has_side_effects=True),
        name="layer",
    )(
        adapter,
        live,
        slots,
        tokens.reshape(steps * rows, width),
        gate_up.transpose(1, 2, 0),
        shrink[0].transpose(0, 2, 1),
        expand[0],
        down,
    )


def build(mesh, ny, nz, block):
    return jax.shard_map(
        functools.partial(shards, ny, nz, block),
        mesh=mesh,
        in_specs=(
            P(None, None, "tensor"),
            P("tensor", None, "pool"),
            P("pool", "tensor"),
            P("pool", None, "tensor", None),
            P("pool", None, "tensor", None),
            P(),
            P(),
            P(),
        ),
        out_specs=P(None, "pool", "tensor"),
        check_vma=False,
    )


def solution(mesh):
    return build(mesh, 8, 8, 128)
```

```python
import functools

import jax
import jax.numpy as jnp
from jax import lax
from jax.experimental import pallas as pl
from jax.experimental.pallas import tpu as pltpu
from jax.sharding import PartitionSpec as P

NBLK = 2
STEPS = 2
NSB = STEPS * NBLK
CORES = 2
WIN = 512
MESH = pl.DeviceIdType.MESH
F32 = jnp.float32
BF16 = jnp.bfloat16


class Exchange:
    def __init__(self, ssem, rsem, phase, me, peers, dev):
        self.ssem, self.rsem, self.phase = ssem, rsem, phase
        self.me, self.peers, self.dev = me, peers, dev

    def copy(self, peer, src, dst, source):
        return pltpu.make_async_remote_copy(
            src_ref=src(peer),
            dst_ref=dst(source),
            send_sem=self.ssem.at[self.phase, peer],
            recv_sem=self.rsem.at[self.phase, source],
            device_id=self.dev(peer),
            device_id_type=MESH,
        )

    def start(self, src, dst):
        self.src, self.dst = src, dst
        for peer in self.peers:
            self.copy(peer, src, dst, self.me).start()

    def wait_from(self, peer):
        self.copy(peer, self.src, self.dst, peer).wait_recv()

    def wait_recv(self):
        for peer in self.peers:
            self.wait_from(peer)

    def wait_send(self):
        for peer in self.peers:
            self.copy(peer, self.src, self.dst, self.me).wait_send()


def nt(a, b):
    return lax.dot_general(a, b, (((1,), (1,)), ((), ())), preferred_element_type=F32)


def kernel(
    ny, nz, block,
    adapter_ref, live_ref, slot_ref, tok_h, w_h, s_h, e_h, d_h, out_ref,
    tok, w, sh, ev, dn,
    sp, srx, sy, sz, pb, brx, bsum,
    e1y, e1z, sel0, sel1, e2y0, e2y1, e2z0, e2z1, ets, erx, ecat, hid,
    fy, by, my, ay, hy, dy, accy, qy, uy,
    fz, bz, mz, az, hz, dz, accz, qz, uz,
    ssem, rsem, lsem, ysend, yrecv, zsend, zrecv,
):
    nt_ = lax.axis_size("tensor")
    p = lax.axis_index("pool")
    t = lax.axis_index("tensor")
    y = lax.div(p, nz)
    z = lax.rem(p, nz)
    rows_t = tok.shape[0] // nt_
    ranks = s_h.shape[1]
    units = w_h.shape[1]
    step_rows = tok.shape[0] // STEPS
    grp = step_rows // (ny * nz)
    span = nz * units
    zshift = nz.bit_length() - 1

    nx = nt_ // CORES
    x = lax.div(t, CORES)
    core = lax.rem(t, CORES)
    width = dn.shape[1]
    hw = width // 2
    hops = [0] + sorted(range(1, nx), key=lambda d: min(d, nx - d))
    chips = [lax.rem(x + d, nx) for d in hops]
    ypeers = [lax.rem(y + k, ny) for k in range(1, ny)]
    zpeers = [lax.rem(z + k, nz) for k in range(1, nz)]
    other = CORES * x + (CORES - 1 - core)
    tpeers = [other] + [
        CORES * c + lax.rem(core + i, CORES) for c in chips[1:] for i in range(CORES)
    ]

    def ydev(i):
        return (i * nz + z, t)

    def zdev(i):
        return (y * nz + i, t)

    def tdev(i):
        return (p, i)

    def win(zi):
        return pl.multiple_of(lax.div(zi * units, 128) * 128, 128)

    barrier = pltpu.get_barrier_semaphore()
    for peers, dev in ((ypeers, ydev), (zpeers, zdev), (tpeers, tdev)):
        for i in peers:
            pl.semaphore_signal(barrier, inc=1, device_id=dev(i), device_id_type=MESH)

    loads = [
        pltpu.make_async_copy(s_h.at[0], sh.at[pl.ds(0, ranks)], lsem.at[0]),
        pltpu.make_async_copy(s_h.at[1], sh.at[pl.ds(ranks, ranks)], lsem.at[1]),
        pltpu.make_async_copy(tok_h, tok, lsem.at[2]),
        pltpu.make_async_copy(w_h, w, lsem.at[3]),
        pltpu.make_async_copy(d_h, dn, lsem.at[4]),
        pltpu.make_async_copy(
            e_h.at[0, :, pl.ds(pl.multiple_of(y * span, 128), span)], e1y.at[y], lsem.at[5]
        ),
    ]
    ecopies = [
        pltpu.make_async_copy(
            e_h.at[1, :, pl.ds(i * span, span)], ev.at[i], lsem.at[6 + i]
        )
        for i in range(ny)
    ]
    for c in ecopies + loads:
        c.start()

    def on_y(phase):
        return Exchange(ssem, rsem, phase, y, ypeers, ydev)

    def on_z(phase):
        return Exchange(ssem, rsem, phase, z, zpeers, zdev)

    def on_t(phase):
        return Exchange(ssem, rsem, phase, t, tpeers, tdev)

    x_e1y, x_e1z = on_y(0), on_z(1)
    x_s, x_sy, x_sz = on_t(2), on_y(3), on_z(4)
    x_b = [on_t(5), on_t(6)]
    x_e2y, x_e2z = [on_z(7), on_z(8)], [on_y(9), on_y(10)]
    x_et, x_h = on_t(11), on_t(12)
    x_qy, x_qz = [on_z(13), on_z(14)], [on_y(15), on_y(16)]

    for c in ecopies:
        c.wait()
    pl.semaphore_wait(barrier, (ny - 1) + (nz - 1) + (nt_ - 1))

    x_e1y.start(
        lambda i: e_h.at[0, :, pl.ds(pl.multiple_of(i * span, 128), span)],
        lambda m: e1y.at[m],
    )
    x_e1z.start(lambda i: ev.at[:, :, pl.ds(win(i), WIN)], lambda m: e1z.at[m])
    own_z = pltpu.make_async_copy(
        ev.at[:, :, pl.ds(win(z), WIN)], e1z.at[z], lsem.at[6 + ny]
    )
    own_z.start()

    for c in loads[:3]:
        c.wait()
    s_part = nt(tok[...], sh[...])
    for i in range(nt_):
        sp[i] = s_part[i * rows_t:(i + 1) * rows_t]
    x_s.start(lambda i: sp.at[i], lambda m: srx.at[m])

    loads[3].wait()

    def base(k):
        part = nt(tok[...], w[k]).astype(BF16)
        for i in range(nt_):
            pb[k, i] = part[i * rows_t:(i + 1) * rows_t]
        x_b[k].start(lambda i: pb.at[k, i], lambda m: brx.at[k, m])

    base(0)

    x_s.wait_recv()
    total = sp[t]
    for i in tpeers:
        total = total + srx[i]
    sy[y] = total.astype(BF16)
    x_sy.start(lambda i: sy.at[y], lambda m: sy.at[m])

    base(1)

    slots = [slot_ref[adapter_ref[i // NBLK, i % NBLK]] for i in range(NSB)]
    yo = [lax.shift_right_logical(s, zshift) for s in slots]
    zo = [lax.bitwise_and(s, nz - 1) for s in slots]
    mine = lax.div(t * rows_t, block)
    my_slot = slot_ref[adapter_ref[lax.div(mine, NBLK), lax.rem(mine, NBLK)]]
    my_yo = lax.shift_right_logical(my_slot, zshift)
    my_zo = lax.bitwise_and(my_slot, nz - 1)

    e2y, e2z = (e2y0, e2y1), (e2z0, e2z1)
    loads[5].wait()
    x_e1y.wait_recv()
    for step in range(STEPS):
        part = pl.ds(step * NBLK, NBLK)
        for i in range(step * NBLK, (step + 1) * NBLK):
            sel0[i] = e1y[yo[i]]
        x_e2y[step].start(
            lambda i, part=part: sel0.at[part, :, pl.ds(win(i), WIN)],
            lambda m, step=step: e2y[step].at[m],
        )
    own_z.wait()
    x_e1z.wait_recv()
    for step in range(STEPS):
        part = pl.ds(step * NBLK, NBLK)
        for i in range(step * NBLK, (step + 1) * NBLK):
            sel1[i] = e1z[zo[i]]
        x_e2z[step].start(
            lambda i, part=part: sel1.at[part, i],
            lambda m, step=step: e2z[step].at[m],
        )
    x_sy.wait_recv()
    sz[z] = sy[my_yo]
    x_sz.start(lambda i: sz.at[z], lambda m: sz.at[m])
    for step in range(STEPS):
        part = pl.ds(step * NBLK, NBLK)
        e2y[step][z] = sel0[part, :, pl.ds(win(z), WIN)]
        e2z[step][y] = sel1[part, y]

    for k in range(2):
        x_b[k].wait_recv()
        total = pb[k, t].astype(F32)
        for i in tpeers:
            total = total + brx[k, i].astype(F32)
        bsum[k] = total

    x_et.src = lambda i: ets.at[lax.div(i * rows_t, block)]
    x_et.dst = lambda m: erx.at[m]
    x_h.src, x_h.dst = (lambda i: hid.at[t]), (lambda m: hid.at[m])
    t_half = nt_ // STEPS
    my_step = lax.div(t, t_half)
    rank_t = ranks // nt_

    def hidden_rows():
        erx[t] = ets[mine]
        x_sz.wait_recv()
        shrunk = sz[my_zo]
        x_et.wait_recv()
        for k in range(2):
            for i in range(nt_):
                ecat[pl.ds(k * ranks + i * rank_t, rank_t)] = erx[i, k].astype(F32)
        second = ecat[...]
        rolled = pltpu.roll(second, WIN - 64, axis=1)
        odd = lax.rem(z, 2) == 1
        second = jnp.where(odd, rolled, second).astype(BF16)
        lane = lax.broadcasted_iota(jnp.int32, shrunk.shape, 1)
        zero = jnp.zeros_like(shrunk)
        gate = jnp.dot(
            jnp.where(lane < ranks, shrunk, zero), second, preferred_element_type=F32
        )
        up = jnp.dot(
            jnp.where(lane < ranks, zero, shrunk), second, preferred_element_type=F32
        )
        gate = bsum[0] + gate[:, :units]
        up = bsum[1] + up[:, :units]
        hid[t] = (gate / (1.0 + jnp.exp(-gate)) * up).astype(BF16)
        x_h.start(x_h.src, x_h.dst)

    for step in range(STEPS):
        x_e2y[step].wait_recv()
        for i in range(NBLK):
            ets[step * NBLK + i, 0] = e2y[step][zo[step * NBLK + i], i]
        x_e2z[step].wait_recv()
        for i in range(NBLK):
            ets[step * NBLK + i, 1] = e2z[step][yo[step * NBLK + i], i]
        for peer in tpeers:

            @pl.when(lax.div(peer, t_half) == step)
            def _(peer=peer):
                x_et.copy(peer, x_et.src, x_et.dst, t).start()

        pl.when(my_step == step)(hidden_rows)

    loads[4].wait()
    gps = nx // STEPS
    ypg = ny // gps
    rows_g = CORES * rows_t
    part_y = nz * grp
    part_z = ypg * grp
    ri = lax.broadcasted_iota(jnp.int32, (rows_g, rows_g), 0)
    ci = lax.broadcasted_iota(jnp.int32, (rows_g, rows_g), 1)
    gbits = grp.bit_length() - 1
    ybits = ypg.bit_length() - 1
    low = lax.bitwise_and(ri, grp - 1)
    yy = lax.bitwise_and(lax.shift_right_logical(ri, gbits), ypg - 1)
    zz = lax.shift_right_logical(ri, gbits + ybits)
    perm = jnp.where(ci == yy * part_y + zz * grp + low, 1.0, 0.0).astype(BF16)

    def project(chip, step):
        for i in range(CORES):
            source = CORES * chip + i

            @pl.when(source != t)
            def _(source=source):
                x_h.wait_from(source)

        h = hid[pl.ds(CORES * chip, CORES)].reshape(rows_g, units)
        group = lax.rem(chip, gps)
        first = group * ypg
        part = jnp.dot(h, dn[:, :hw], preferred_element_type=F32)
        for i in range(ypg):
            piece = part[i * part_y:(i + 1) * part_y]
            fy[step, first + i] = piece
            by[step, first + i] = piece.astype(BF16)
        h = jnp.dot(perm, h, preferred_element_type=F32).astype(BF16)
        part = jnp.dot(h, dn[:, hw:], preferred_element_type=F32)
        place = pl.ds(pl.multiple_of(group * part_z, part_z), part_z)
        for i in range(nz):
            piece = part[i * part_z:(i + 1) * part_z]
            fz[step, i, place] = piece
            bz[step, i, place] = piece.astype(BF16)

    class Ring:
        def __init__(self, n, me, dev, full, short, merged, far, half, near, send, recv):
            self.n, self.me, self.dev, self.full = n, me, dev, full
            self.short, self.merged, self.far = short, merged, far
            self.half, self.near, self.send, self.recv = half, near, send, recv
            self.first = {1: (), 2: (4,), 8: (0, 1, 2, 3, 4, 5)}[n]
            self.second = {1: (), 2: (), 8: (6, 7)}[n]

        def at(self, offset):
            return lax.rem(self.me + offset + self.n, self.n)

        def copy(self, step, kind):
            hh = hw // 2
            hop, src, dst = {
                0: (1, lambda: self.short.at[step, self.at(3)], self.far.at[step, 0]),
                1: (-1, lambda: self.short.at[step, self.at(-3)], self.far.at[step, 1]),
                2: (2, lambda: self.short.at[step, self.at(4), :, pl.ds(0, hh)],
                    self.half.at[step, 0]),
                3: (-2, lambda: self.short.at[step, self.at(4), :, pl.ds(hh, hh)],
                    self.half.at[step, 1]),
                4: (1, lambda: self.short.at[step, self.at(1)], self.near.at[step, 0]),
                5: (-1, lambda: self.short.at[step, self.at(-1)], self.near.at[step, 1]),
                6: (2, lambda: self.merged.at[step, 0], self.near.at[step, 2]),
                7: (-2, lambda: self.merged.at[step, 1], self.near.at[step, 3]),
            }[kind]
            return pltpu.make_async_remote_copy(
                src_ref=src(),
                dst_ref=dst,
                send_sem=self.send.at[step, kind],
                recv_sem=self.recv.at[step, kind],
                device_id=self.dev(self.at(hop)),
                device_id_type=MESH,
            )

        def start(self, step):
            for kind in self.first:
                self.copy(step, kind).start()

        def merge(self, step):
            hh = hw // 2
            for side in range(len(self.second)):
                self.copy(step, side).wait_recv()
                self.copy(step, 2 + side).wait_recv()
                total = self.full[step, self.at((2, -2)[side])]
                total = total + self.far[step, side].astype(F32)
                more = self.half[step, side].astype(F32)
                left, right = total[:, :hh], total[:, hh:]
                if side == 0:
                    left = left + more
                else:
                    right = right + more
                self.merged[step, side, :, pl.ds(0, hh)] = left.astype(BF16)
                self.merged[step, side, :, pl.ds(hh, hh)] = right.astype(BF16)
                self.copy(step, 6 + side).start()

        def total(self, step):
            total = self.full[step, self.me]
            for kind in self.first[4:] + self.second if self.n == 8 else self.first:
                self.copy(step, kind).wait_recv()
                total = total + self.near[step, kind - 4].astype(F32)
            return total

        def wait_send(self):
            for step in range(STEPS):
                for kind in self.first + self.second:
                    self.copy(step, kind).wait_send()

    ring_y = Ring(ny, y, ydev, fy, by, my, ay, hy, dy, ysend, yrecv)
    ring_z = Ring(nz, z, zdev, fz, bz, mz, az, hz, dz, zsend, zrecv)
    late = x >= gps
    if gps == 2:
        order = [
            (jnp.where(late, nx - 1 - x, x), jnp.where(late, x - gps, 1 - x)),
            (jnp.where(late, x, nx - 1 - x), jnp.where(late, 5 - x, x + gps)),
        ]
    else:
        order = [(0,), (1,)]

    def finish(step):
        accy[...] = ring_y.total(step)
        for i in range(nz):
            qy[step, i] = accy[pl.ds(i * grp, grp), :]
        x_qy[step].start(
            lambda i: qy.at[step, i], lambda m: uy.at[step, m]
        )
        accz[...] = ring_z.total(step)
        for i in range(ny):
            qz[step, i] = accz[pl.ds(i * grp, grp), :]
        x_qz[step].start(
            lambda i: qz.at[step, i], lambda m: uz.at[step, m]
        )

    for chip in order[0]:
        project(chip, 0)
    ring_y.start(0)
    ring_z.start(0)
    project(order[1][0], 1)
    ring_y.merge(0)
    ring_z.merge(0)
    for chip in order[1][1:]:
        project(chip, 1)
    ring_y.start(1)
    ring_z.start(1)
    finish(0)
    ring_y.merge(1)
    ring_z.merge(1)
    finish(1)

    first = p * grp
    place = lax.rem(first, block) + lax.broadcasted_iota(jnp.int32, (grp, hw), 0)
    owner = lax.div(first, block)
    for step in range(STEPS):
        keep = place < live_ref[step, owner]
        for half, (xq, q, u, peers, me) in enumerate(
            ((x_qy, qy, uy, zpeers, z), (x_qz, qz, uz, ypeers, y))
        ):
            total = q[step, me]
            for i in peers:
                xq[step].wait_from(i)
                total = total + u[step, i]
            out_ref[step, :, half * hw:(half + 1) * hw] = jnp.where(
                keep, total, 0.0
            ).astype(BF16)

    for e in (x_e1y, x_e1z, x_s, *x_b, x_sy, x_sz, *x_e2y, *x_e2z, x_et, x_h,
              *x_qy, *x_qz, ring_y, ring_z):
        e.wait_send()


def ring_scratch(n, other, grp, hw):
    rows = other * grp
    vmem = pltpu.VMEM
    return [
        vmem((STEPS, n, rows, hw), F32),
        vmem((STEPS, n, rows, hw), BF16),
        vmem((STEPS, 2, rows, hw), BF16),
        vmem((STEPS, 2, rows, hw), BF16),
        vmem((STEPS, 2, rows, hw // 2), BF16),
        vmem((STEPS, 4, rows, hw), BF16),
        vmem((rows, hw), F32),
        vmem((STEPS, other, grp, hw), F32),
        vmem((STEPS, other, grp, hw), F32),
    ]


def shards(ny, nz, block, tokens, gate_up, down, shrink, expand, adapter, live, slots):
    steps, rows, width = tokens.shape
    units = gate_up.shape[2]
    ranks = shrink.shape[3]
    rank_t = expand.shape[2]
    n_t = lax.axis_size("tensor")
    rows_t = steps * rows // n_t
    grp = rows // (ny * nz)
    span = nz * units
    hw = width // 2
    any_spec = pl.BlockSpec(memory_space=pl.ANY)
    smem = pl.BlockSpec(memory_space=pltpu.SMEM)
    vmem = pltpu.VMEM
    scratch = [
        vmem((steps * rows, width), BF16),
        vmem((2, units, width), BF16),
        vmem((2 * ranks, width), BF16),
        vmem((ny, rank_t, span), BF16),
        vmem((units, width), BF16),
        vmem((n_t, rows_t, 2 * ranks), F32),
        vmem((n_t, rows_t, 2 * ranks), F32),
        vmem((ny, rows_t, 2 * ranks), BF16),
        vmem((nz, rows_t, 2 * ranks), BF16),
        vmem((2, n_t, rows_t, units), BF16),
        vmem((2, n_t, rows_t, units), BF16),
        vmem((2, rows_t, units), F32),
        vmem((ny, rank_t, span), BF16),
        vmem((nz, ny, rank_t, WIN), BF16),
        vmem((NSB, rank_t, span), BF16),
        vmem((NSB, ny, rank_t, WIN), BF16),
        vmem((nz, NBLK, rank_t, WIN), BF16),
        vmem((nz, NBLK, rank_t, WIN), BF16),
        vmem((ny, NBLK, rank_t, WIN), BF16),
        vmem((ny, NBLK, rank_t, WIN), BF16),
        vmem((NSB, 2, rank_t, WIN), BF16),
        vmem((n_t, 2, rank_t, WIN), BF16),
        vmem((2 * ranks, WIN), F32),
        vmem((n_t, rows_t, units), BF16),
        *ring_scratch(ny, nz, grp, hw),
        *ring_scratch(nz, ny, grp, hw),
        pltpu.SemaphoreType.DMA((17, max(ny, nz, n_t))),
        pltpu.SemaphoreType.DMA((17, max(ny, nz, n_t))),
        pltpu.SemaphoreType.DMA((7 + ny,)),
        pltpu.SemaphoreType.DMA((steps, 8)),
        pltpu.SemaphoreType.DMA((steps, 8)),
        pltpu.SemaphoreType.DMA((steps, 8)),
        pltpu.SemaphoreType.DMA((steps, 8)),
    ]
    return pl.pallas_call(
        functools.partial(kernel, ny, nz, block),
        out_shape=jax.ShapeDtypeStruct((steps, grp, width), BF16),
        in_specs=[smem, smem, smem] + [any_spec] * 5,
        out_specs=pl.BlockSpec(memory_space=pltpu.VMEM),
        scratch_shapes=scratch,
        compiler_params=pltpu.CompilerParams(collective_id=0, has_side_effects=True),
        name="layer",
    )(
        adapter,
        live,
        slots,
        tokens.reshape(steps * rows, width),
        gate_up.transpose(1, 2, 0),
        shrink[0].transpose(0, 2, 1),
        expand[0],
        down,
    )


def build(mesh, ny, nz, block):
    return jax.shard_map(
        functools.partial(shards, ny, nz, block),
        mesh=mesh,
        in_specs=(
            P(None, None, "tensor"),
            P("tensor", None, "pool"),
            P("pool", "tensor"),
            P("pool", None, "tensor", None),
            P("pool", None, "tensor", None),
            P(),
            P(),
            P(),
        ),
        out_specs=P(None, "pool", "tensor"),
        check_vma=False,
    )


def solution(mesh):
    return build(mesh, 8, 8, 128)
```

```python
import functools

import jax
import jax.numpy as jnp
from jax import lax
from jax.experimental import pallas as pl
from jax.experimental.pallas import tpu as pltpu
from jax.sharding import PartitionSpec as P

NBLK = 2
STEPS = 2
NSB = STEPS * NBLK
CORES = 2
WIN = 512
MESH = pl.DeviceIdType.MESH
F32 = jnp.float32
BF16 = jnp.bfloat16


class Exchange:
    def __init__(self, ssem, rsem, phase, me, peers, dev):
        self.ssem, self.rsem, self.phase = ssem, rsem, phase
        self.me, self.peers, self.dev = me, peers, dev

    def copy(self, peer, src, dst, source):
        return pltpu.make_async_remote_copy(
            src_ref=src(peer),
            dst_ref=dst(source),
            send_sem=self.ssem.at[self.phase, peer],
            recv_sem=self.rsem.at[self.phase, source],
            device_id=self.dev(peer),
            device_id_type=MESH,
        )

    def start(self, src, dst):
        self.src, self.dst = src, dst
        for peer in self.peers:
            self.copy(peer, src, dst, self.me).start()

    def wait_from(self, peer):
        self.copy(peer, self.src, self.dst, peer).wait_recv()

    def wait_recv(self):
        for peer in self.peers:
            self.wait_from(peer)

    def wait_send(self):
        for peer in self.peers:
            self.copy(peer, self.src, self.dst, self.me).wait_send()


def nt(a, b):
    return lax.dot_general(a, b, (((1,), (1,)), ((), ())), preferred_element_type=F32)


def kernel(
    ny, nz, block,
    adapter_ref, live_ref, slot_ref, tok_h, w_h, s_h, e_h, d_h, out_ref,
    tok, w, sh, ev, dn,
    sp, srx, sy, sz, pb0, brx0, pb1, brx1, bsum,
    e1y, e1z, sel0, sel1, e2y, e2z, ets, erx, ecat, hid,
    fy, by, my, ay, hy, dy, accy, qy, uy,
    fz, bz, mz, az, hz, dz, accz, qz, uz,
    ssem, rsem, lsem, ysend, yrecv, zsend, zrecv,
):
    nt_ = lax.axis_size("tensor")
    p = lax.axis_index("pool")
    t = lax.axis_index("tensor")
    y = lax.div(p, nz)
    z = lax.rem(p, nz)
    rows_t = tok.shape[0] // nt_
    ranks = s_h.shape[1]
    units = w_h.shape[1]
    step_rows = tok.shape[0] // STEPS
    grp = step_rows // (ny * nz)
    span = nz * units
    zshift = nz.bit_length() - 1

    nx = nt_ // CORES
    x = lax.div(t, CORES)
    core = lax.rem(t, CORES)
    width = dn.shape[1]
    hw = width // 2
    hops = [0] + sorted(range(1, nx), key=lambda d: min(d, nx - d))
    chips = [lax.rem(x + d, nx) for d in hops]
    ypeers = [lax.rem(y + k, ny) for k in range(1, ny)]
    zpeers = [lax.rem(z + k, nz) for k in range(1, nz)]
    other = CORES * x + (CORES - 1 - core)
    tpeers = [other] + [
        CORES * c + lax.rem(core + i, CORES) for c in chips[1:] for i in range(CORES)
    ]

    def ydev(i):
        return (i * nz + z, t)

    def zdev(i):
        return (y * nz + i, t)

    def tdev(i):
        return (p, i)

    def win(zi):
        return pl.multiple_of(lax.div(zi * units, 128) * 128, 128)

    barrier = pltpu.get_barrier_semaphore()
    for peers, dev in ((ypeers, ydev), (zpeers, zdev), (tpeers, tdev)):
        for i in peers:
            pl.semaphore_signal(barrier, inc=1, device_id=dev(i), device_id_type=MESH)

    loads = [
        pltpu.make_async_copy(s_h.at[0], sh.at[pl.ds(0, ranks)], lsem.at[0]),
        pltpu.make_async_copy(s_h.at[1], sh.at[pl.ds(ranks, ranks)], lsem.at[1]),
        pltpu.make_async_copy(tok_h, tok, lsem.at[2]),
        pltpu.make_async_copy(w_h, w, lsem.at[3]),
        pltpu.make_async_copy(d_h, dn, lsem.at[4]),
        pltpu.make_async_copy(
            e_h.at[0, :, pl.ds(pl.multiple_of(y * span, 128), span)], e1y.at[y], lsem.at[5]
        ),
    ]
    ecopies = [
        pltpu.make_async_copy(
            e_h.at[1, :, pl.ds(i * span, span)], ev.at[i], lsem.at[6 + i]
        )
        for i in range(ny)
    ]
    for c in ecopies + loads:
        c.start()

    def on_y(phase):
        return Exchange(ssem, rsem, phase, y, ypeers, ydev)

    def on_z(phase):
        return Exchange(ssem, rsem, phase, z, zpeers, zdev)

    def on_t(phase):
        return Exchange(ssem, rsem, phase, t, tpeers, tdev)

    x_e1y, x_e1z = on_y(0), on_z(1)
    x_s, x_sy, x_sz = on_t(2), on_y(3), on_z(4)
    x_b = [on_t(5), on_t(6)]
    x_e2y, x_e2z = on_z(7), on_y(8)
    x_et, x_h = [on_t(11), on_t(17)], on_t(12)
    if nx == 4:
        pair = x + 1 - 2 * lax.rem(x, 2)
        x_h.peers = [other] + [
            CORES * c + lax.rem(core + i, CORES)
            for c in (pair, lax.rem(x + 2, nx), nx - 1 - x)
            for i in range(CORES)
        ]
    x_qy, x_qz = [on_z(13), on_z(14)], [on_y(15), on_y(16)]

    for c in ecopies:
        c.wait()
    pl.semaphore_wait(barrier, (ny - 1) + (nz - 1) + (nt_ - 1))

    x_e1y.start(
        lambda i: e_h.at[0, :, pl.ds(pl.multiple_of(i * span, 128), span)],
        lambda m: e1y.at[m],
    )
    x_e1z.start(lambda i: ev.at[:, :, pl.ds(win(i), WIN)], lambda m: e1z.at[m])
    own_z = pltpu.make_async_copy(
        ev.at[:, :, pl.ds(win(z), WIN)], e1z.at[z], lsem.at[6 + ny]
    )
    own_z.start()

    for c in loads[:3]:
        c.wait()
    s_part = nt(tok[...], sh[...])
    for i in range(nt_):
        sp[i] = s_part[i * rows_t:(i + 1) * rows_t]
    x_s.start(lambda i: sp.at[i], lambda m: srx.at[m])

    loads[3].wait()

    pb, brx = (pb0, pb1), (brx0, brx1)

    def base(k):
        part = nt(tok[...], w[k]).astype(pb[k].dtype)
        for i in range(nt_):
            pb[k][i] = part[i * rows_t:(i + 1) * rows_t]
        x_b[k].start(lambda i: pb[k].at[i], lambda m: brx[k].at[m])

    base(0)

    x_s.wait_recv()
    total = sp[t]
    for i in tpeers:
        total = total + srx[i]
    sy[y] = total.astype(BF16)
    x_sy.start(lambda i: sy.at[y], lambda m: sy.at[m])

    base(1)

    slots = [slot_ref[adapter_ref[i // NBLK, i % NBLK]] for i in range(NSB)]
    yo = [lax.shift_right_logical(s, zshift) for s in slots]
    zo = [lax.bitwise_and(s, nz - 1) for s in slots]
    mine = lax.div(t * rows_t, block)
    my_slot = slot_ref[adapter_ref[lax.div(mine, NBLK), lax.rem(mine, NBLK)]]
    my_yo = lax.shift_right_logical(my_slot, zshift)
    my_zo = lax.bitwise_and(my_slot, nz - 1)

    loads[5].wait()
    x_e1y.wait_recv()
    for i in range(NSB):
        sel0[i] = e1y[yo[i]]
    x_e2y.start(lambda i: sel0.at[:, :, pl.ds(win(i), WIN)], lambda m: e2y.at[m])
    own_z.wait()
    x_e1z.wait_recv()
    for i in range(NSB):
        sel1[i] = e1z[zo[i]]
    x_e2z.start(lambda i: sel1.at[:, i], lambda m: e2z.at[m])
    x_sy.wait_recv()
    sz[z] = sy[my_yo]
    x_sz.start(lambda i: sz.at[z], lambda m: sz.at[m])
    e2y[z] = sel0[:, :, pl.ds(win(z), WIN)]
    e2z[y] = sel1[:, y]

    for k in range(2):
        x_b[k].wait_recv()
        total = pb[k][t].astype(F32)
        for i in tpeers:
            total = total + brx[k][i].astype(F32)
        bsum[k] = total

    x_h.src, x_h.dst = (lambda i: hid.at[t]), (lambda m: hid.at[m])
    my_step = lax.div(t, nt_ // STEPS)
    rank_t = ranks // nt_

    def hidden_rows():
        for k in range(2):
            erx[k, t] = ets[k, mine]
        x_sz.wait_recv()
        shrunk = sz[my_zo]
        for k in range(2):
            x_et[k].wait_recv()
        for k in range(2):
            for i in range(nt_):
                ecat[pl.ds(k * ranks + i * rank_t, rank_t)] = erx[k, i].astype(F32)
        second = ecat[...]
        rolled = pltpu.roll(second, WIN - 64, axis=1)
        odd = lax.rem(z, 2) == 1
        second = jnp.where(odd, rolled, second).astype(BF16)
        lane = lax.broadcasted_iota(jnp.int32, shrunk.shape, 1)
        zero = jnp.zeros_like(shrunk)
        gate = jnp.dot(
            jnp.where(lane < ranks, shrunk, zero), second, preferred_element_type=F32
        )
        up = jnp.dot(
            jnp.where(lane < ranks, zero, shrunk), second, preferred_element_type=F32
        )
        gate = bsum[0] + gate[:, :units]
        up = bsum[1] + up[:, :units]
        hid[t] = (gate / (1.0 + jnp.exp(-gate)) * up).astype(BF16)
        x_h.start(x_h.src, x_h.dst)

    for k, (e, ref, own) in enumerate(((x_e2y, e2y, zo), (x_e2z, e2z, yo))):
        e.wait_recv()
        for i in range(NSB):
            ets[k, i] = ref[own[i], i]
        x_et[k].start(
            lambda i, k=k: ets.at[k, lax.div(i * rows_t, block)],
            lambda m, k=k: erx.at[k, m],
        )
    hidden_rows()

    loads[4].wait()
    gps = nx // STEPS
    ypg = ny // gps
    rows_g = CORES * rows_t
    part_y = nz * grp
    part_z = ypg * grp
    ri = lax.broadcasted_iota(jnp.int32, (rows_g, rows_g), 0)
    ci = lax.broadcasted_iota(jnp.int32, (rows_g, rows_g), 1)
    gbits = grp.bit_length() - 1
    ybits = ypg.bit_length() - 1
    low = lax.bitwise_and(ri, grp - 1)
    yy = lax.bitwise_and(lax.shift_right_logical(ri, gbits), ypg - 1)
    zz = lax.shift_right_logical(ri, gbits + ybits)
    perm = jnp.where(ci == yy * part_y + zz * grp + low, 1.0, 0.0).astype(BF16)

    def project(chip, step):
        for i in range(CORES):
            source = CORES * chip + i

            @pl.when(source != t)
            def _(source=source):
                x_h.wait_from(source)

        h = hid[pl.ds(CORES * chip, CORES)].reshape(rows_g, units)
        group = lax.rem(chip, gps)
        first = group * ypg
        part = jnp.dot(h, dn[:, :hw], preferred_element_type=F32)
        for i in range(ypg):
            piece = part[i * part_y:(i + 1) * part_y]
            fy[step, first + i] = piece
            by[step, first + i] = piece.astype(BF16)
        h = jnp.dot(perm, h, preferred_element_type=F32).astype(BF16)
        part = jnp.dot(h, dn[:, hw:], preferred_element_type=F32)
        place = pl.ds(pl.multiple_of(group * part_z, part_z), part_z)
        for i in range(nz):
            piece = part[i * part_z:(i + 1) * part_z]
            fz[step, i, place] = piece
            bz[step, i, place] = piece.astype(BF16)

    class Ring:
        def __init__(self, n, me, dev, full, short, merged, far, half, near, send, recv):
            self.n, self.me, self.dev, self.full = n, me, dev, full
            self.short, self.merged, self.far = short, merged, far
            self.half, self.near, self.send, self.recv = half, near, send, recv
            self.first = {1: (), 2: (4,), 8: (0, 1, 2, 3, 4, 5)}[n]
            self.second = {1: (), 2: (), 8: (6, 7)}[n]

        def at(self, offset):
            return lax.rem(self.me + offset + self.n, self.n)

        def copy(self, step, kind):
            hh = hw // 2
            hop, src, dst = {
                0: (1, lambda: self.short.at[step, self.at(3)], self.far.at[step, 0]),
                1: (-1, lambda: self.short.at[step, self.at(-3)], self.far.at[step, 1]),
                2: (2, lambda: self.short.at[step, self.at(4), :, pl.ds(0, hh)],
                    self.half.at[step, 0]),
                3: (-2, lambda: self.short.at[step, self.at(4), :, pl.ds(hh, hh)],
                    self.half.at[step, 1]),
                4: (1, lambda: self.short.at[step, self.at(1)], self.near.at[step, 0]),
                5: (-1, lambda: self.short.at[step, self.at(-1)], self.near.at[step, 1]),
                6: (2, lambda: self.merged.at[step, 0], self.near.at[step, 2]),
                7: (-2, lambda: self.merged.at[step, 1], self.near.at[step, 3]),
            }[kind]
            return pltpu.make_async_remote_copy(
                src_ref=src(),
                dst_ref=dst,
                send_sem=self.send.at[step, kind],
                recv_sem=self.recv.at[step, kind],
                device_id=self.dev(self.at(hop)),
                device_id_type=MESH,
            )

        def start(self, step):
            for kind in self.first:
                self.copy(step, kind).start()

        def merge(self, step):
            hh = hw // 2
            for side in range(len(self.second)):
                self.copy(step, side).wait_recv()
                self.copy(step, 2 + side).wait_recv()
                total = self.full[step, self.at((2, -2)[side])]
                total = total + self.far[step, side].astype(F32)
                more = self.half[step, side].astype(F32)
                left, right = total[:, :hh], total[:, hh:]
                if side == 0:
                    left = left + more
                else:
                    right = right + more
                self.merged[step, side, :, pl.ds(0, hh)] = left.astype(BF16)
                self.merged[step, side, :, pl.ds(hh, hh)] = right.astype(BF16)
                self.copy(step, 6 + side).start()

        def total(self, step):
            total = self.full[step, self.me]
            for kind in self.first[4:] + self.second if self.n == 8 else self.first:
                self.copy(step, kind).wait_recv()
                total = total + self.near[step, kind - 4].astype(F32)
            return total

        def wait_send(self):
            for step in range(STEPS):
                for kind in self.first + self.second:
                    self.copy(step, kind).wait_send()

    ring_y = Ring(ny, y, ydev, fy, by, my, ay, hy, dy, ysend, yrecv)
    ring_z = Ring(nz, z, zdev, fz, bz, mz, az, hz, dz, zsend, zrecv)
    order = [(x,), (1 - x,)] if gps == 1 else [
        (x, x + 1 - 2 * lax.rem(x, 2)), (nx - 1 - x, lax.rem(x + gps, nx))
    ]

    def finish(step):
        accy[...] = ring_y.total(step)
        for i in range(nz):
            qy[step, i] = accy[pl.ds(i * grp, grp), :]
        x_qy[step].start(
            lambda i: qy.at[step, i], lambda m: uy.at[step, m]
        )
        accz[...] = ring_z.total(step)
        for i in range(ny):
            qz[step, i] = accz[pl.ds(i * grp, grp), :]
        x_qz[step].start(
            lambda i: qz.at[step, i], lambda m: uz.at[step, m]
        )

    for turn in range(STEPS):
        for chip in order[turn]:
            project(chip, turn)
        ring_y.start(turn)
        ring_z.start(turn)
    for turn in range(STEPS):
        ring_y.merge(turn)
        ring_z.merge(turn)
    for turn in range(STEPS):
        finish(turn)

    first = p * grp
    place = lax.rem(first, block) + lax.broadcasted_iota(jnp.int32, (grp, hw), 0)
    owner = lax.div(first, block)
    for turn in range(STEPS):
        step = lax.rem(my_step + turn, STEPS)
        keep = place < live_ref[step, owner]
        for half, (xq, q, u, peers, me) in enumerate(
            ((x_qy, qy, uy, zpeers, z), (x_qz, qz, uz, ypeers, y))
        ):
            total = q[turn, me]
            for i in peers:
                xq[turn].wait_from(i)
                total = total + u[turn, i]
            out_ref[step, :, half * hw:(half + 1) * hw] = jnp.where(
                keep, total, 0.0
            ).astype(BF16)

    for e in (x_e1y, x_e1z, x_s, *x_b, x_sy, x_sz, x_e2y, x_e2z, *x_et, x_h,
              *x_qy, *x_qz, ring_y, ring_z):
        e.wait_send()


def ring_scratch(n, other, grp, hw):
    rows = other * grp
    vmem = pltpu.VMEM
    return [
        vmem((STEPS, n, rows, hw), F32),
        vmem((STEPS, n, rows, hw), BF16),
        vmem((STEPS, 2, rows, hw), BF16),
        vmem((STEPS, 2, rows, hw), BF16),
        vmem((STEPS, 2, rows, hw // 2), BF16),
        vmem((STEPS, 4, rows, hw), BF16),
        vmem((rows, hw), F32),
        vmem((STEPS, other, grp, hw), F32),
        vmem((STEPS, other, grp, hw), F32),
    ]


def shards(ny, nz, block, tokens, gate_up, down, shrink, expand, adapter, live, slots):
    steps, rows, width = tokens.shape
    units = gate_up.shape[2]
    ranks = shrink.shape[3]
    rank_t = expand.shape[2]
    n_t = lax.axis_size("tensor")
    rows_t = steps * rows // n_t
    grp = rows // (ny * nz)
    span = nz * units
    hw = width // 2
    any_spec = pl.BlockSpec(memory_space=pl.ANY)
    smem = pl.BlockSpec(memory_space=pltpu.SMEM)
    vmem = pltpu.VMEM
    scratch = [
        vmem((steps * rows, width), BF16),
        vmem((2, units, width), BF16),
        vmem((2 * ranks, width), BF16),
        vmem((ny, rank_t, span), BF16),
        vmem((units, width), BF16),
        vmem((n_t, rows_t, 2 * ranks), F32),
        vmem((n_t, rows_t, 2 * ranks), F32),
        vmem((ny, rows_t, 2 * ranks), BF16),
        vmem((nz, rows_t, 2 * ranks), BF16),
        vmem((n_t, rows_t, units), F32),
        vmem((n_t, rows_t, units), F32),
        vmem((n_t, rows_t, units), BF16),
        vmem((n_t, rows_t, units), BF16),
        vmem((2, rows_t, units), F32),
        vmem((ny, rank_t, span), BF16),
        vmem((nz, ny, rank_t, WIN), BF16),
        vmem((NSB, rank_t, span), BF16),
        vmem((NSB, ny, rank_t, WIN), BF16),
        vmem((nz, NSB, rank_t, WIN), BF16),
        vmem((ny, NSB, rank_t, WIN), BF16),
        vmem((2, NSB, rank_t, WIN), BF16),
        vmem((2, n_t, rank_t, WIN), BF16),
        vmem((2 * ranks, WIN), F32),
        vmem((n_t, rows_t, units), BF16),
        *ring_scratch(ny, nz, grp, hw),
        *ring_scratch(nz, ny, grp, hw),
        pltpu.SemaphoreType.DMA((18, max(ny, nz, n_t))),
        pltpu.SemaphoreType.DMA((18, max(ny, nz, n_t))),
        pltpu.SemaphoreType.DMA((7 + ny,)),
        pltpu.SemaphoreType.DMA((steps, 8)),
        pltpu.SemaphoreType.DMA((steps, 8)),
        pltpu.SemaphoreType.DMA((steps, 8)),
        pltpu.SemaphoreType.DMA((steps, 8)),
    ]
    return pl.pallas_call(
        functools.partial(kernel, ny, nz, block),
        out_shape=jax.ShapeDtypeStruct((steps, grp, width), BF16),
        in_specs=[smem, smem, smem] + [any_spec] * 5,
        out_specs=pl.BlockSpec(memory_space=pltpu.VMEM),
        scratch_shapes=scratch,
        compiler_params=pltpu.CompilerParams(collective_id=0, has_side_effects=True),
        name="layer",
    )(
        adapter,
        live,
        slots,
        tokens.reshape(steps * rows, width),
        gate_up.transpose(1, 2, 0),
        shrink[0].transpose(0, 2, 1),
        expand[0],
        down,
    )


def build(mesh, ny, nz, block):
    return jax.shard_map(
        functools.partial(shards, ny, nz, block),
        mesh=mesh,
        in_specs=(
            P(None, None, "tensor"),
            P("tensor", None, "pool"),
            P("pool", "tensor"),
            P("pool", None, "tensor", None),
            P("pool", None, "tensor", None),
            P(),
            P(),
            P(),
        ),
        out_specs=P(None, "pool", "tensor"),
        check_vma=False,
    )


def solution(mesh):
    return build(mesh, 8, 8, 128)
```

```python
import functools

import jax
import jax.numpy as jnp
from jax import lax
from jax.experimental import pallas as pl
from jax.experimental.pallas import tpu as pltpu
from jax.sharding import PartitionSpec as P

NBLK = 2
STEPS = 2
NSB = STEPS * NBLK
CORES = 2
WIN = 512
MESH = pl.DeviceIdType.MESH
F32 = jnp.float32
BF16 = jnp.bfloat16


class Exchange:
    def __init__(self, ssem, rsem, phase, me, peers, dev):
        self.ssem, self.rsem, self.phase = ssem, rsem, phase
        self.me, self.peers, self.dev = me, peers, dev

    def copy(self, peer, src, dst, source):
        return pltpu.make_async_remote_copy(
            src_ref=src(peer),
            dst_ref=dst(source),
            send_sem=self.ssem.at[self.phase, peer],
            recv_sem=self.rsem.at[self.phase, source],
            device_id=self.dev(peer),
            device_id_type=MESH,
        )

    def start(self, src, dst):
        self.src, self.dst = src, dst
        for peer in self.peers:
            self.copy(peer, src, dst, self.me).start()

    def wait_from(self, peer):
        self.copy(peer, self.src, self.dst, peer).wait_recv()

    def wait_recv(self):
        for peer in self.peers:
            self.wait_from(peer)

    def wait_send(self):
        for peer in self.peers:
            self.copy(peer, self.src, self.dst, self.me).wait_send()


def nt(a, b):
    return lax.dot_general(a, b, (((1,), (1,)), ((), ())), preferred_element_type=F32)


def kernel(
    ny, nz, block,
    adapter_ref, live_ref, slot_ref, tok_h, w_h, s_h, e_h, d_h, out_ref,
    tok, w, sh, ev, dn,
    sp, srx, sy, sz, pb0, brx0, pb1, brx1, bsum,
    e1y, e1z, sel0, sel1, e2y, e2z, ets, erx, ecat, hid,
    fy, by, my, ay, hy, dy, accy, qy, uy,
    fz, bz, mz, az, hz, dz, accz, qz, uz,
    ssem, rsem, lsem, ysend, yrecv, zsend, zrecv,
):
    nt_ = lax.axis_size("tensor")
    p = lax.axis_index("pool")
    t = lax.axis_index("tensor")
    y = lax.div(p, nz)
    z = lax.rem(p, nz)
    rows_t = tok.shape[0] // nt_
    ranks = s_h.shape[1]
    units = w_h.shape[1]
    step_rows = tok.shape[0] // STEPS
    grp = step_rows // (ny * nz)
    span = nz * units
    zshift = nz.bit_length() - 1

    nx = nt_ // CORES
    x = lax.div(t, CORES)
    core = lax.rem(t, CORES)
    width = dn.shape[1]
    hw = width // 2
    hops = [0] + sorted(range(1, nx), key=lambda d: min(d, nx - d))
    chips = [lax.rem(x + d, nx) for d in hops]
    ypeers = [lax.rem(y + k, ny) for k in sorted(range(1, ny), key=lambda k: -min(k, ny - k))]
    zpeers = [lax.rem(z + k, nz) for k in sorted(range(1, nz), key=lambda k: -min(k, nz - k))]
    other = CORES * x + (CORES - 1 - core)
    tpeers = [other] + [
        CORES * c + lax.rem(core + i, CORES) for c in chips[1:] for i in range(CORES)
    ]

    def ydev(i):
        return (i * nz + z, t)

    def zdev(i):
        return (y * nz + i, t)

    def tdev(i):
        return (p, i)

    def win(zi):
        return pl.multiple_of(lax.div(zi * units, 128) * 128, 128)

    barrier = pltpu.get_barrier_semaphore()
    for peers, dev in ((ypeers, ydev), (zpeers, zdev), (tpeers, tdev)):
        for i in peers:
            pl.semaphore_signal(barrier, inc=1, device_id=dev(i), device_id_type=MESH)

    loads = [
        pltpu.make_async_copy(s_h.at[0], sh.at[pl.ds(0, ranks)], lsem.at[0]),
        pltpu.make_async_copy(s_h.at[1], sh.at[pl.ds(ranks, ranks)], lsem.at[1]),
        pltpu.make_async_copy(tok_h, tok, lsem.at[2]),
        pltpu.make_async_copy(w_h, w, lsem.at[3]),
        pltpu.make_async_copy(d_h, dn, lsem.at[4]),
        pltpu.make_async_copy(
            e_h.at[0, :, pl.ds(pl.multiple_of(y * span, 128), span)], e1y.at[y], lsem.at[5]
        ),
    ]
    ecopies = [
        pltpu.make_async_copy(
            e_h.at[1, :, pl.ds(i * span, span)], ev.at[i], lsem.at[6 + i]
        )
        for i in range(ny)
    ]
    for c in ecopies + loads:
        c.start()

    def on_y(phase):
        return Exchange(ssem, rsem, phase, y, ypeers, ydev)

    def on_z(phase):
        return Exchange(ssem, rsem, phase, z, zpeers, zdev)

    def on_t(phase):
        return Exchange(ssem, rsem, phase, t, tpeers, tdev)

    x_e1y, x_e1z = on_y(0), on_z(1)
    x_s, x_sy, x_sz = on_t(2), on_y(3), on_z(4)
    x_b = [on_t(5), on_t(6)]
    x_e2y, x_e2z = on_z(7), on_y(8)
    x_et, x_h = [on_t(11), on_t(17)], on_t(12)
    if nx == 4:
        pair = x + 1 - 2 * lax.rem(x, 2)
        x_h.peers = [other] + [
            CORES * c + lax.rem(core + i, CORES)
            for c in (pair, lax.rem(x + 2, nx), nx - 1 - x)
            for i in range(CORES)
        ]
    x_qy, x_qz = [on_z(13), on_z(14)], [on_y(15), on_y(16)]

    for c in ecopies:
        c.wait()
    pl.semaphore_wait(barrier, (ny - 1) + (nz - 1) + (nt_ - 1))

    x_e1y.start(
        lambda i: e_h.at[0, :, pl.ds(pl.multiple_of(i * span, 128), span)],
        lambda m: e1y.at[m],
    )
    x_e1z.start(lambda i: ev.at[:, :, pl.ds(win(i), WIN)], lambda m: e1z.at[m])
    own_z = pltpu.make_async_copy(
        ev.at[:, :, pl.ds(win(z), WIN)], e1z.at[z], lsem.at[6 + ny]
    )
    own_z.start()

    for c in loads[:3]:
        c.wait()
    s_part = nt(tok[...], sh[...])
    for i in range(nt_):
        sp[i] = s_part[i * rows_t:(i + 1) * rows_t]
    x_s.start(lambda i: sp.at[i], lambda m: srx.at[m])

    loads[3].wait()

    pb, brx = (pb0, pb1), (brx0, brx1)

    def base(k):
        part = nt(tok[...], w[k]).astype(pb[k].dtype)
        for i in range(nt_):
            pb[k][i] = part[i * rows_t:(i + 1) * rows_t]
        x_b[k].start(lambda i: pb[k].at[i], lambda m: brx[k].at[m])

    base(0)

    x_s.wait_recv()
    total = sp[t]
    for i in tpeers:
        total = total + srx[i]
    sy[y] = total.astype(BF16)
    x_sy.start(lambda i: sy.at[y], lambda m: sy.at[m])

    base(1)

    slots = [slot_ref[adapter_ref[i // NBLK, i % NBLK]] for i in range(NSB)]
    yo = [lax.shift_right_logical(s, zshift) for s in slots]
    zo = [lax.bitwise_and(s, nz - 1) for s in slots]
    mine = lax.div(t * rows_t, block)
    my_slot = slot_ref[adapter_ref[lax.div(mine, NBLK), lax.rem(mine, NBLK)]]
    my_yo = lax.shift_right_logical(my_slot, zshift)
    my_zo = lax.bitwise_and(my_slot, nz - 1)

    loads[5].wait()
    x_e1y.wait_recv()
    for i in range(NSB):
        sel0[i] = e1y[yo[i]]
    x_e2y.start(lambda i: sel0.at[:, :, pl.ds(win(i), WIN)], lambda m: e2y.at[m])
    own_z.wait()
    x_e1z.wait_recv()
    for i in range(NSB):
        sel1[i] = e1z[zo[i]]
    x_e2z.start(lambda i: sel1.at[:, i], lambda m: e2z.at[m])
    x_sy.wait_recv()
    sz[z] = sy[my_yo]
    x_sz.start(lambda i: sz.at[z], lambda m: sz.at[m])
    e2y[z] = sel0[:, :, pl.ds(win(z), WIN)]
    e2z[y] = sel1[:, y]

    for k in range(2):
        x_b[k].wait_recv()
        total = pb[k][t].astype(F32)
        for i in tpeers:
            total = total + brx[k][i].astype(F32)
        bsum[k] = total

    x_h.src, x_h.dst = (lambda i: hid.at[t]), (lambda m: hid.at[m])
    my_step = lax.div(t, nt_ // STEPS)
    rank_t = ranks // nt_

    def hidden_rows():
        for k in range(2):
            erx[k, t] = ets[k, mine]
        x_sz.wait_recv()
        shrunk = sz[my_zo]
        for k in range(2):
            x_et[k].wait_recv()
        for k in range(2):
            for i in range(nt_):
                ecat[pl.ds(k * ranks + i * rank_t, rank_t)] = erx[k, i].astype(F32)
        second = ecat[...]
        rolled = pltpu.roll(second, WIN - 64, axis=1)
        odd = lax.rem(z, 2) == 1
        second = jnp.where(odd, rolled, second).astype(BF16)
        lane = lax.broadcasted_iota(jnp.int32, shrunk.shape, 1)
        zero = jnp.zeros_like(shrunk)
        gate = jnp.dot(
            jnp.where(lane < ranks, shrunk, zero), second, preferred_element_type=F32
        )
        up = jnp.dot(
            jnp.where(lane < ranks, zero, shrunk), second, preferred_element_type=F32
        )
        gate = bsum[0] + gate[:, :units]
        up = bsum[1] + up[:, :units]
        hid[t] = (gate / (1.0 + jnp.exp(-gate)) * up).astype(BF16)
        x_h.start(x_h.src, x_h.dst)

    for k, (e, ref, own) in enumerate(((x_e2y, e2y, zo), (x_e2z, e2z, yo))):
        e.wait_recv()
        for i in range(NSB):
            ets[k, i] = ref[own[i], i]
        x_et[k].start(
            lambda i, k=k: ets.at[k, lax.div(i * rows_t, block)],
            lambda m, k=k: erx.at[k, m],
        )
    hidden_rows()

    loads[4].wait()
    gps = nx // STEPS
    ypg = ny // gps
    rows_g = CORES * rows_t
    part_y = nz * grp
    part_z = ypg * grp
    ri = lax.broadcasted_iota(jnp.int32, (rows_g, rows_g), 0)
    ci = lax.broadcasted_iota(jnp.int32, (rows_g, rows_g), 1)
    gbits = grp.bit_length() - 1
    ybits = ypg.bit_length() - 1
    low = lax.bitwise_and(ri, grp - 1)
    yy = lax.bitwise_and(lax.shift_right_logical(ri, gbits), ypg - 1)
    zz = lax.shift_right_logical(ri, gbits + ybits)
    perm = jnp.where(ci == yy * part_y + zz * grp + low, 1.0, 0.0).astype(BF16)

    def project(chip, step):
        for i in range(CORES):
            source = CORES * chip + i

            @pl.when(source != t)
            def _(source=source):
                x_h.wait_from(source)

        h = hid[pl.ds(CORES * chip, CORES)].reshape(rows_g, units)
        group = lax.rem(chip, gps)
        first = group * ypg
        part = jnp.dot(h, dn[:, :hw], preferred_element_type=F32)
        for i in range(ypg):
            piece = part[i * part_y:(i + 1) * part_y]
            fy[step, first + i] = piece
            by[step, first + i] = piece.astype(BF16)
        h = jnp.dot(perm, h, preferred_element_type=F32).astype(BF16)
        part = jnp.dot(h, dn[:, hw:], preferred_element_type=F32)
        place = pl.ds(pl.multiple_of(group * part_z, part_z), part_z)
        for i in range(nz):
            piece = part[i * part_z:(i + 1) * part_z]
            fz[step, i, place] = piece
            bz[step, i, place] = piece.astype(BF16)

    class Ring:
        def __init__(self, n, me, dev, full, short, merged, far, half, near, send, recv):
            self.n, self.me, self.dev, self.full = n, me, dev, full
            self.short, self.merged, self.far = short, merged, far
            self.half, self.near, self.send, self.recv = half, near, send, recv
            self.first = {1: (), 2: (4,), 8: (0, 1, 2, 3, 4, 5)}[n]
            self.second = {1: (), 2: (), 8: (6, 7)}[n]

        def at(self, offset):
            return lax.rem(self.me + offset + self.n, self.n)

        def copy(self, step, kind):
            hh = hw // 2
            hop, src, dst = {
                0: (1, lambda: self.short.at[step, self.at(3)], self.far.at[step, 0]),
                1: (-1, lambda: self.short.at[step, self.at(-3)], self.far.at[step, 1]),
                2: (2, lambda: self.short.at[step, self.at(4), :, pl.ds(0, hh)],
                    self.half.at[step, 0]),
                3: (-2, lambda: self.short.at[step, self.at(4), :, pl.ds(hh, hh)],
                    self.half.at[step, 1]),
                4: (1, lambda: self.short.at[step, self.at(1)], self.near.at[step, 0]),
                5: (-1, lambda: self.short.at[step, self.at(-1)], self.near.at[step, 1]),
                6: (2, lambda: self.merged.at[step, 0], self.near.at[step, 2]),
                7: (-2, lambda: self.merged.at[step, 1], self.near.at[step, 3]),
            }[kind]
            return pltpu.make_async_remote_copy(
                src_ref=src(),
                dst_ref=dst,
                send_sem=self.send.at[step, kind],
                recv_sem=self.recv.at[step, kind],
                device_id=self.dev(self.at(hop)),
                device_id_type=MESH,
            )

        def start(self, step):
            for kind in self.first:
                self.copy(step, kind).start()

        def merge(self, step):
            hh = hw // 2
            for side in range(len(self.second)):
                self.copy(step, side).wait_recv()
                self.copy(step, 2 + side).wait_recv()
                total = self.full[step, self.at((2, -2)[side])]
                total = total + self.far[step, side].astype(F32)
                more = self.half[step, side].astype(F32)
                left, right = total[:, :hh], total[:, hh:]
                if side == 0:
                    left = left + more
                else:
                    right = right + more
                self.merged[step, side, :, pl.ds(0, hh)] = left.astype(BF16)
                self.merged[step, side, :, pl.ds(hh, hh)] = right.astype(BF16)
                self.copy(step, 6 + side).start()

        def total(self, step):
            total = self.full[step, self.me]
            for kind in self.first[4:] + self.second if self.n == 8 else self.first:
                self.copy(step, kind).wait_recv()
                total = total + self.near[step, kind - 4].astype(F32)
            return total

        def wait_send(self):
            for step in range(STEPS):
                for kind in self.first + self.second:
                    self.copy(step, kind).wait_send()

    ring_y = Ring(ny, y, ydev, fy, by, my, ay, hy, dy, ysend, yrecv)
    ring_z = Ring(nz, z, zdev, fz, bz, mz, az, hz, dz, zsend, zrecv)
    order = [(x,), (1 - x,)] if gps == 1 else [
        (x, x + 1 - 2 * lax.rem(x, 2)), (nx - 1 - x, lax.rem(x + gps, nx))
    ]

    def finish(step):
        accy[...] = ring_y.total(step)
        for i in range(nz):
            qy[step, i] = accy[pl.ds(i * grp, grp), :]
        x_qy[step].start(
            lambda i: qy.at[step, i], lambda m: uy.at[step, m]
        )
        accz[...] = ring_z.total(step)
        for i in range(ny):
            qz[step, i] = accz[pl.ds(i * grp, grp), :]
        x_qz[step].start(
            lambda i: qz.at[step, i], lambda m: uz.at[step, m]
        )

    for turn in range(STEPS):
        for chip in order[turn]:
            project(chip, turn)
        ring_y.start(turn)
        ring_z.start(turn)
    for turn in range(STEPS):
        ring_y.merge(turn)
        ring_z.merge(turn)
    for turn in range(STEPS):
        finish(turn)

    first = p * grp
    place = lax.rem(first, block) + lax.broadcasted_iota(jnp.int32, (grp, hw), 0)
    owner = lax.div(first, block)
    for turn in range(STEPS):
        step = lax.rem(my_step + turn, STEPS)
        keep = place < live_ref[step, owner]
        for half, (xq, q, u, peers, me) in enumerate(
            ((x_qy, qy, uy, zpeers, z), (x_qz, qz, uz, ypeers, y))
        ):
            total = q[turn, me]
            for i in peers:
                xq[turn].wait_from(i)
                total = total + u[turn, i]
            out_ref[step, :, half * hw:(half + 1) * hw] = jnp.where(
                keep, total, 0.0
            ).astype(BF16)

    for e in (x_e1y, x_e1z, x_s, *x_b, x_sy, x_sz, x_e2y, x_e2z, *x_et, x_h,
              *x_qy, *x_qz, ring_y, ring_z):
        e.wait_send()


def ring_scratch(n, other, grp, hw):
    rows = other * grp
    vmem = pltpu.VMEM
    return [
        vmem((STEPS, n, rows, hw), F32),
        vmem((STEPS, n, rows, hw), BF16),
        vmem((STEPS, 2, rows, hw), BF16),
        vmem((STEPS, 2, rows, hw), BF16),
        vmem((STEPS, 2, rows, hw // 2), BF16),
        vmem((STEPS, 4, rows, hw), BF16),
        vmem((rows, hw), F32),
        vmem((STEPS, other, grp, hw), F32),
        vmem((STEPS, other, grp, hw), F32),
    ]


def shards(ny, nz, block, tokens, gate_up, down, shrink, expand, adapter, live, slots):
    steps, rows, width = tokens.shape
    units = gate_up.shape[2]
    ranks = shrink.shape[3]
    rank_t = expand.shape[2]
    n_t = lax.axis_size("tensor")
    rows_t = steps * rows // n_t
    grp = rows // (ny * nz)
    span = nz * units
    hw = width // 2
    any_spec = pl.BlockSpec(memory_space=pl.ANY)
    smem = pl.BlockSpec(memory_space=pltpu.SMEM)
    vmem = pltpu.VMEM
    scratch = [
        vmem((steps * rows, width), BF16),
        vmem((2, units, width), BF16),
        vmem((2 * ranks, width), BF16),
        vmem((ny, rank_t, span), BF16),
        vmem((units, width), BF16),
        vmem((n_t, rows_t, 2 * ranks), F32),
        vmem((n_t, rows_t, 2 * ranks), F32),
        vmem((ny, rows_t, 2 * ranks), BF16),
        vmem((nz, rows_t, 2 * ranks), BF16),
        vmem((n_t, rows_t, units), F32),
        vmem((n_t, rows_t, units), F32),
        vmem((n_t, rows_t, units), BF16),
        vmem((n_t, rows_t, units), BF16),
        vmem((2, rows_t, units), F32),
        vmem((ny, rank_t, span), BF16),
        vmem((nz, ny, rank_t, WIN), BF16),
        vmem((NSB, rank_t, span), BF16),
        vmem((NSB, ny, rank_t, WIN), BF16),
        vmem((nz, NSB, rank_t, WIN), BF16),
        vmem((ny, NSB, rank_t, WIN), BF16),
        vmem((2, NSB, rank_t, WIN), BF16),
        vmem((2, n_t, rank_t, WIN), BF16),
        vmem((2 * ranks, WIN), F32),
        vmem((n_t, rows_t, units), BF16),
        *ring_scratch(ny, nz, grp, hw),
        *ring_scratch(nz, ny, grp, hw),
        pltpu.SemaphoreType.DMA((18, max(ny, nz, n_t))),
        pltpu.SemaphoreType.DMA((18, max(ny, nz, n_t))),
        pltpu.SemaphoreType.DMA((7 + ny,)),
        pltpu.SemaphoreType.DMA((steps, 8)),
        pltpu.SemaphoreType.DMA((steps, 8)),
        pltpu.SemaphoreType.DMA((steps, 8)),
        pltpu.SemaphoreType.DMA((steps, 8)),
    ]
    return pl.pallas_call(
        functools.partial(kernel, ny, nz, block),
        out_shape=jax.ShapeDtypeStruct((steps, grp, width), BF16),
        in_specs=[smem, smem, smem] + [any_spec] * 5,
        out_specs=pl.BlockSpec(memory_space=pltpu.VMEM),
        scratch_shapes=scratch,
        compiler_params=pltpu.CompilerParams(collective_id=0, has_side_effects=True),
        name="layer",
    )(
        adapter,
        live,
        slots,
        tokens.reshape(steps * rows, width),
        gate_up.transpose(1, 2, 0),
        shrink[0].transpose(0, 2, 1),
        expand[0],
        down,
    )


def build(mesh, ny, nz, block):
    return jax.shard_map(
        functools.partial(shards, ny, nz, block),
        mesh=mesh,
        in_specs=(
            P(None, None, "tensor"),
            P("tensor", None, "pool"),
            P("pool", "tensor"),
            P("pool", None, "tensor", None),
            P("pool", None, "tensor", None),
            P(),
            P(),
            P(),
        ),
        out_specs=P(None, "pool", "tensor"),
        check_vma=False,
    )


def solution(mesh):
    return build(mesh, 8, 8, 128)
```
